128 devices in a mesh: ex: 16 (over y, x), ey: 8 (over z, core).
Axes of the slice: x: 4, y: 4, z: 4, core: 2. Of those that a mesh axis runs over, the one named last changes fastest.
Arguments:
- tokens: bfloat16 [8192, 3584], P(('ex', 'ey')), may hold values from -6 to 6
- route_ids: int32 [8192, 8], P(('ex', 'ey')), may hold values from 0 to 127, all different within a row; in each aligned block of 64 rows (0 to 63, 64 to 127, ...) at most 8 rows name the same one
- route_weight: bfloat16 [8192, 8], P(('ex', 'ey')), may hold values from 0.19921875 to 1
- w_gate: bfloat16 [128, 3584, 1024], P(('ex', 'ey')), may hold values from -0.09375 to 0.09375
- w_up: bfloat16 [128, 3584, 1024], P(('ex', 'ey')), may hold values from -0.09375 to 0.09375
- w_down: bfloat16 [128, 1024, 3584], P(('ex', 'ey')), may hold values from -0.1875 to 0.1875
- shared_gate: bfloat16 [3584, 2048], P(None, 'ex'), may hold values from -0.09375 to 0.09375
- shared_up: bfloat16 [3584, 2048], P(None, 'ex'), may hold values from -0.09375 to 0.09375
- shared_down: bfloat16 [2048, 3584], P('ex'), may hold values from -0.125 to 0.125
Outputs:
- layer_out: bfloat16 [8192, 3584], P(('ex', 'ey'))
The draws below stay inside these ranges and needn't reach their ends.
Inputs may be any that keep to these rules, and one draw needn't show every extreme that they name: `route_ids`: each row names 8 different experts; within the rows of one device no expert is named more than 8 times, a bound that some block reaches.
All inputs are finite; a program needn't handle non-finite values.
Results may differ from the reference program's by a relative error of at most 0.009.
Values may be sent and summed in bfloat16 or wider, within the bound.
A program may use at most 128 MiB of HBM per device.

```python
import math
import jax
import jax.numpy as jnp
import numpy as np
from jax import lax

D = 3584
FF = 1024
SFF = 2048
TOP = 8
TOK_DEV = 64
EXPERTS = 128
TOKENS = 8192
MOST = 8
N_EX = 16


def block_levels(key, dims, shards, low, largest):
    factor_of = 1.0
    for dim, shards_of in shards:
        draws = jax.random.uniform(jax.random.fold_in(jax.random.fold_in(key, 6), dim), (shards_of,), jnp.float32, low / len(shards), largest / len(shards))
        factor_of = factor_of * jnp.repeat(jnp.exp(draws), dims[dim] // shards_of).reshape((-1,) + (1,) * (len(dims) - 1 - dim))
    return factor_of


def deal_out(own_key, own, number, rows, number_of, top, most, lean):
    sequence = jax.random.permutation(own_key, number_of)
    heavy_load, common = portions_of(number_of, rows * top, most, lean, True), portions_of(number_of, rows * top, most, lean, False)
    places = jnp.arange(number_of)

    def named(lengths, turn):
        used = int((lengths > 0).sum())
        fixed = max(1, used // 4)
        moved = fixed + (places - fixed + turn * (used - fixed)) % max(1, number_of - fixed)
        return jnp.zeros((number_of,), jnp.int32).at[sequence[jnp.where(places < fixed, places, moved)]].set(jnp.asarray(lengths, jnp.int32))

    lengths = jnp.where(number % 4 == 0, named(heavy_load, number // 4), named(common, number - number // 4 - 1))
    mixed = jax.random.permutation(jax.random.fold_in(own, 3), number_of)
    giver, receiver = mixed[0:number_of // 2 * 2:2], mixed[1:number_of // 2 * 2:2]
    slack = jnp.minimum(lengths[giver] - 1, most - lengths[receiver]) // 2
    slack = jnp.where((giver == sequence[0]) | (receiver == sequence[0]) | (lengths[receiver] == 0), 0, jnp.maximum(slack, 0))
    moved = jax.random.randint(jax.random.fold_in(own, 4), (number_of // 2,), 0, 1 << 20) % (slack + 1)
    lengths = lengths.at[giver].add(-moved).at[receiver].add(moved)
    labels = jnp.searchsorted(jnp.cumsum(lengths), jnp.arange(rows * top), side="right").astype(jnp.int32)
    listing = labels.reshape(top, rows).T
    listing = listing[jax.random.permutation(jax.random.fold_in(own, 1), rows)]
    turn = jax.random.randint(jax.random.fold_in(own, 2), (rows, 1), 0, top)
    return jnp.take_along_axis(listing, (jnp.arange(top)[None, :] + turn) % top, axis=1)


def portions_of(number_of, total, most, skew, full):
    loads = [(1 << 20) // math.isqrt(standing ** skew) + 1 for standing in range(1, number_of + 1)]
    largest = most if full else min(most, max(-(-total // number_of), total * loads[0] // sum(loads)))
    least = 1 if total - largest >= number_of - 1 else 0
    holding, surplus = [largest] + [least] * (number_of - 1), total - largest - least * (number_of - 1)
    while surplus > 0:
        candidates = [i for i in range(1, number_of) if holding[i] < largest] or [i for i in range(1, number_of) if holding[i] < most]
        mass, left = sum([loads[i] for i in candidates]), surplus
        for i in candidates:
            addition = min(most - holding[i], max(1, left * loads[i] // mass), surplus)
            holding[i] = holding[i] + addition
            surplus = surplus - addition
    return np.array(holding)


def centred(stream_key, extent, spread, most, cuts=(), kind=jnp.bfloat16):
    array = jax.random.normal(stream_key, extent, jnp.float32) * spread
    if len(cuts) > 0:
        array = block_levels(stream_key, extent, cuts, -0.22, 0.18) * array
    return jnp.clip(array, min=-most, max=most).astype(kind)


def setup_inputs(seed: int = 0) -> dict:
    splits = jax.random.split(jax.random.key(seed), 10)
    tokens = centred(splits[0], (TOKENS, D), 1.0, 6.0, ((0, 128),))
    route_ids_keys = jax.random.split(jax.random.fold_in(splits[1], 1), TOKENS // TOK_DEV)
    route_ids_turns = jax.random.permutation(jax.random.fold_in(splits[1], 3), TOKENS // TOK_DEV)
    route_ids = jax.vmap(lambda own, number: deal_out(jax.random.fold_in(splits[1], 2), own, number, TOK_DEV, EXPERTS, TOP, MOST, 2))(route_ids_keys, route_ids_turns).reshape((TOKENS, TOP))
    route_weight = jnp.clip(jnp.exp(math.log(1.0) - 1.6133518 * jax.random.uniform(splits[2], (TOKENS, TOP), jnp.float32) ** block_levels(splits[2], (TOKENS, TOP), ((0, 128),), -0.2, 0.2)), 0.19921875, 1.0).astype(jnp.bfloat16)
    w_gate = centred(splits[3], (EXPERTS, D, FF), D ** -0.5, 0.09375, ((0, 128),))
    w_up = centred(splits[4], (EXPERTS, D, FF), D ** -0.5, 0.09375, ((0, 128),))
    w_down = centred(splits[5], (EXPERTS, FF, D), FF ** -0.5, 0.1875, ((0, 128),))
    shared_gate = centred(splits[6], (D, SFF), D ** -0.5, 0.09375, ((1, 16),))
    shared_up = centred(splits[7], (D, SFF), D ** -0.5, 0.09375, ((1, 16),))
    shared_down = centred(splits[8], (SFF, D), SFF ** -0.5, 0.125, ((0, 16),))
    return dict(tokens=tokens, route_ids=route_ids, route_weight=route_weight, w_gate=w_gate, w_up=w_up, w_down=w_down, shared_gate=shared_gate, shared_up=shared_up, shared_down=shared_down)


def swiglu(chosen, gate_weight, up_weight, down_weight):
    gate_act = jnp.dot(chosen, gate_weight, preferred_element_type=jnp.float32)
    up_act = jnp.dot(chosen, up_weight, preferred_element_type=jnp.float32)
    hidden = (jax.nn.silu(gate_act) * up_act).astype(jnp.bfloat16)
    return jnp.dot(hidden, down_weight, preferred_element_type=jnp.float32)


def reference(tokens, route_ids, route_weight, w_gate, w_up, w_down, shared_gate, shared_up, shared_down):
    flat_ids = route_ids.reshape(-1).astype(jnp.int32)
    slot_count = TOKENS * TOP
    onehot = (flat_ids[:, None] == jnp.arange(EXPERTS, dtype=jnp.int32)[None, :]).astype(jnp.int32)
    blocks = onehot.reshape(EXPERTS, TOK_DEV * TOP, EXPERTS)
    before = jnp.cumsum(blocks, axis=1) - blocks
    slot_rank = jnp.sum(before * blocks, axis=2).reshape(-1).astype(jnp.int32)
    source = (jnp.arange(slot_count, dtype=jnp.int32) // (TOK_DEV * TOP)).astype(jnp.int32)
    capacity = EXPERTS * MOST
    slot_place = (flat_ids * capacity + source * MOST + slot_rank).astype(jnp.int32)
    token_of = (jnp.arange(slot_count, dtype=jnp.int32) // TOP).astype(jnp.int32)
    lookup = jnp.full((EXPERTS * capacity,), TOKENS, jnp.int32).at[slot_place].set(token_of)
    padded = jnp.concatenate([tokens, jnp.zeros((1, D), tokens.dtype)], axis=0)

    def run_expert(expert):
        picked = lax.dynamic_slice(lookup, (expert * capacity,), (capacity,))
        chosen = padded[picked]
        return swiglu(chosen, w_gate[expert], w_up[expert], w_down[expert]).astype(jnp.bfloat16)

    results = lax.map(run_expert, jnp.arange(EXPERTS, dtype=jnp.int32))
    slot_out = results.reshape(-1, D)[slot_place]
    weighted = slot_out.astype(jnp.float32).reshape(TOKENS, TOP, D) * route_weight.astype(jnp.float32)[:, :, None]
    routed = jnp.sum(weighted, axis=1)
    group = SFF // N_EX
    shared = jnp.zeros((TOKENS, D), jnp.float32)
    for index in range(N_EX):
        low = index * group
        part_value = swiglu(tokens, shared_gate[:, low:low + group], shared_up[:, low:low + group], shared_down[low:low + group, :])
        shared = shared + part_value.astype(jnp.bfloat16).astype(jnp.float32)
    return (shared + routed).astype(jnp.bfloat16)
```

```python
import functools

import jax
import jax.numpy as jnp
from jax import lax
from jax.experimental import pallas as pl
from jax.experimental.pallas import tpu as pltpu
from jax.sharding import PartitionSpec as P

MESH = pl.DeviceIdType.MESH
F32 = jnp.float32
BF16 = jnp.bfloat16
LAG = 2
W = 256


def dot(a, b):
    return jnp.dot(a, b, preferred_element_type=F32)


class Place:
    def __init__(self):
        self.ex = lax.axis_index("ex")
        self.ey = lax.axis_index("ey")
        self.x = lax.rem(self.ex, 4)
        self.y = lax.div(self.ex, 4)

    def along_x(self, step):
        return (self.y * 4 + lax.rem(self.x + step, 4), self.ey)

    def along_y(self, step):
        return (lax.rem(self.y + step, 4) * 4 + self.x, self.ey)

    def along_ey(self, step):
        return (self.ex, lax.rem(self.ey + step, 8))

    def greet(self):
        barrier = pltpu.get_barrier_semaphore()
        partners = [self.along_x(s) for s in (1, 2, 3)]
        partners += [self.along_y(s) for s in (1, 2, 3)]
        partners += [self.along_ey(s) for s in range(1, 8)]
        for partner in partners:
            pl.semaphore_signal(barrier, inc=1, device_id=partner, device_id_type=MESH)
        pl.semaphore_wait(barrier, len(partners))


def remote(src, dst, send, recv, partner):
    return pltpu.make_async_remote_copy(
        src_ref=src, dst_ref=dst, send_sem=send, recv_sem=recv, device_id=partner, device_id_type=MESH
    )


def dispatch_kernel(
    pairs,
    tok, ids, weight, w_gate, w_up, s_gate, s_up,
    h_out, hs_out, comb,
    ag, snd, rcv, acc_g, acc_u, gate_v, up_v, sgu, meta, metas, place_t, acc_s,
    load_sem, m1_send, m1_recv, m2_send, m2_recv, p1_send, p1_recv, p2_send, p2_recv, z_send, z_recv,
):
    at = Place()
    x, y, ey = at.x, at.y, at.ey

    def loads(i):
        rows = pl.ds(pl.multiple_of(i * 2 * W, 2 * W), 2 * W)
        return (
            pltpu.make_async_copy(w_gate.at[0, rows], gate_v.at[i], load_sem.at[0, i]),
            pltpu.make_async_copy(w_up.at[0, rows], up_v.at[i], load_sem.at[1, i]),
            pltpu.make_async_copy(s_gate.at[rows], sgu.at[i, :, pl.ds(0, 128)], load_sem.at[2, i]),
            pltpu.make_async_copy(s_up.at[rows], sgu.at[i, :, pl.ds(128, 128)], load_sem.at[3, i]),
        )

    def start_loads(i, carry):
        for copy in loads(i):
            copy.start()
        return carry

    lax.fori_loop(0, pairs, start_loads, 0)

    lane = lax.broadcasted_iota(jnp.int32, (64, 128), 1)
    hits = [ids[:, k : k + 1] == lane for k in range(8)]
    named = sum(jnp.where(hit, 1.0, 0.0) for hit in hits)
    lower = lax.broadcasted_iota(jnp.int32, (64, 64), 0) > lax.broadcasted_iota(jnp.int32, (64, 64), 1)
    before = dot(jnp.where(lower, 1.0, 0.0).astype(BF16), named.astype(BF16))
    info = jnp.zeros((64, 128), F32)
    for k in range(8):
        rank = jnp.sum(jnp.where(hits[k], before, 0.0), axis=1, keepdims=True)
        code = ids[:, k : k + 1].astype(F32) * 32.0 + rank
        info = jnp.where(lane == k, code, info)
        info = jnp.where(lane == 8 + k, weight[:, k : k + 1].astype(F32), info)
    meta[...] = info
    metas[y, x] = info

    def own(c, carry):
        columns = pl.ds(pl.multiple_of(c * W, W), W)
        ag[c, y, x] = tok[:, columns]
        return carry

    lax.fori_loop(0, 2 * pairs, own, 0)

    at.greet()

    def first(c, half, s):
        partner = at.along_x(s) if half == 0 else at.along_y(s)
        columns = pl.ds(pl.multiple_of(c * W, W), W)
        return remote(tok.at[:, columns], ag.at[c, y, x], p1_send.at[c, s - 1], p1_recv.at[c, s - 1], partner)

    def second(c, half, s):
        if half == 0:
            return remote(ag.at[c, y], ag.at[c, y], p2_send.at[c, s - 1], p2_recv.at[c, s - 1], at.along_y(s))
        return remote(ag.at[c, :, x], ag.at[c, :, x], p2_send.at[c, s - 1], p2_recv.at[c, s - 1], at.along_x(s))

    def cross(c, s):
        target = lax.rem(ey + s, 8)
        return remote(snd.at[c, target], rcv.at[c, ey], z_send.at[c, s - 1], z_recv.at[c, s - 1], at.along_ey(s))

    def meta_first(s):
        return remote(meta, metas.at[y, x], m1_send.at[s - 1], m1_recv.at[s - 1], at.along_x(s))

    def meta_second(s):
        return remote(metas.at[y], metas.at[y], m2_send.at[s - 1], m2_recv.at[s - 1], at.along_y(s))

    def start_first(i):
        for half in (0, 1):
            for s in (2, 1, 3):
                first(2 * i + half, half, s).start()

    def start_second(i):
        for half in (0, 1):
            for s in (1, 2, 3):
                first(2 * i + half, half, s).wait_recv()
            for s in (2, 1, 3):
                second(2 * i + half, half, s).start()

    for s in (2, 1, 3):
        meta_first(s).start()
    start_first(0)
    start_first(1)
    for s in (1, 2, 3):
        meta_first(s).wait_recv()
    for s in (2, 1, 3):
        meta_second(s).start()
    start_second(0)

    def clear(r, carry):
        rows = pl.ds(pl.multiple_of(r * 64, 64), 64)
        acc_g[rows] = jnp.zeros((64, 1024), F32)
        acc_u[rows] = jnp.zeros((64, 1024), F32)
        acc_s[rows] = jnp.zeros((64, 256), F32)
        return carry

    lax.fori_loop(0, 16, clear, 0)

    for s in (1, 2, 3):
        meta_second(s).wait_recv()

    def matrices(q, carry):
        known = metas[q].reshape(256, 128)
        slot = lax.broadcasted_iota(jnp.int32, (256, 256), 1).astype(F32)
        source = lax.div(lax.broadcasted_iota(jnp.int32, (256, 1), 0), 64)
        shift = (source * 8 - at.ex * 256).astype(F32)
        total = jnp.zeros((256, 256), F32)
        for k in range(8):
            hit = (known[:, k : k + 1] + shift) == slot
            total = jnp.where(hit, known[:, 8 + k : 9 + k], total)
        comb[q] = total.astype(BF16)
        place_t[q] = jnp.where(total > 0.0, 1.0, 0.0).T.astype(BF16)
        return carry

    lax.fori_loop(0, 4, matrices, 0)

    def compact(i):
        for half in (0, 1):
            c = 2 * i + half
            for s in (1, 2, 3):
                second(c, half, s).wait_recv()

            def quad(q, carry):
                rows = dot(place_t[q], ag[c, q].reshape(256, W)).astype(BF16)
                snd[c, :, pl.ds(pl.multiple_of(q * 32, 32), 32)] = rows.reshape(8, 32, W)
                return carry

            lax.fori_loop(0, 4, quad, 0)
            rcv[c, ey] = snd[c, ey]
            for s in (4, 3, 5, 2, 6, 1, 7):
                cross(c, s).start()

    def shared(i):
        for copy in loads(i)[2:]:
            copy.wait()

        def quad(q, carry):
            rows = pl.ds(pl.multiple_of(q * 256, 256), 256)
            acc_s[rows] += dot(ag[2 * i, q].reshape(256, W), sgu[i, :W]) + dot(
                ag[2 * i + 1, q].reshape(256, W), sgu[i, W:]
            )
            return carry

        lax.fori_loop(0, 4, quad, 0)

    def expert(i):
        for copy in loads(i)[:2]:
            copy.wait()
        for half in (0, 1):
            for s in range(1, 8):
                cross(2 * i + half, s).wait_recv()

        def tile(m, carry):
            rows = pl.ds(pl.multiple_of(m * 256, 256), 256)
            blocks = pl.ds(2 * m, 2)
            left = rcv[2 * i, blocks].reshape(256, W)
            right = rcv[2 * i + 1, blocks].reshape(256, W)
            acc_g[rows] += dot(left, gate_v[i, :W]) + dot(right, gate_v[i, W:])
            acc_u[rows] += dot(left, up_v[i, :W]) + dot(right, up_v[i, W:])
            return carry

        lax.fori_loop(0, 4, tile, 0)

    def step(i, carry):
        @pl.when(i + 2 < pairs)
        def _():
            start_first(i + 2)

        @pl.when(i + 1 < pairs)
        def _():
            start_second(i + 1)

        @pl.when(i < pairs)
        def _():
            compact(i)
            shared(i)

        @pl.when(i >= LAG)
        def _():
            expert(i - LAG)

        return carry

    lax.fori_loop(0, pairs + LAG, step, 0)

    def finish(r, carry):
        rows = pl.ds(pl.multiple_of(r * 64, 64), 64)
        h_out[rows] = (jax.nn.silu(acc_g[rows]) * acc_u[rows]).astype(BF16)
        both = acc_s[rows]
        hs_out[rows] = (jax.nn.silu(both[:, :128]) * both[:, 128:]).astype(BF16)
        return carry

    lax.fori_loop(0, 16, finish, 0)

    for s in (1, 2, 3):
        meta_first(s).wait_send()
        meta_second(s).wait_send()

    def drain(i, carry):
        for half in (0, 1):
            c = 2 * i + half
            for s in (1, 2, 3):
                first(c, half, s).wait_send()
                second(c, half, s).wait_send()
            for s in range(1, 8):
                cross(c, s).wait_send()
        return carry

    lax.fori_loop(0, pairs, drain, 0)


def return_kernel(
    pairs,
    h, hs, comb, w_down, s_down,
    out,
    down_v, sd_v, snd, rcv, part, got1, half_sum, got2,
    load_sem, z_send, z_recv, r1_send, r1_recv, r2_send, r2_recv,
):
    at = Place()
    x, y, ey = at.x, at.y, at.ey

    def loads(i):
        columns = pl.ds(pl.multiple_of(i * 2 * W, 2 * W), 2 * W)
        return (
            pltpu.make_async_copy(w_down.at[0, :, columns], down_v.at[i], load_sem.at[0, i]),
            pltpu.make_async_copy(s_down.at[:, columns], sd_v.at[i], load_sem.at[1, i]),
        )

    def start_loads(i, carry):
        for copy in loads(i):
            copy.start()
        return carry

    lax.fori_loop(0, pairs, start_loads, 0)
    at.greet()

    def cross(c, s):
        target = lax.rem(ey + s, 8)
        return remote(snd.at[c, target], rcv.at[c, ey], z_send.at[c, s - 1], z_recv.at[c, s - 1], at.along_ey(s))

    def first(c, half, s):
        if half == 0:
            src, partner = part.at[c, lax.rem(y + s, 4)], at.along_y(s)
        else:
            src, partner = part.at[c, :, lax.rem(x + s, 4)], at.along_x(s)
        return remote(src, got1.at[c, s - 1], r1_send.at[c, s - 1], r1_recv.at[c, s - 1], partner)

    def second(c, half, s):
        if half == 0:
            src, partner = half_sum.at[c, lax.rem(x + s, 4)], at.along_x(s)
        else:
            src, partner = half_sum.at[c, lax.rem(y + s, 4)], at.along_y(s)
        return remote(src, got2.at[c, s - 1], r2_send.at[c, s - 1], r2_recv.at[c, s - 1], partner)

    def down(i):
        loads(i)[0].wait()

        def tile(m, carry):
            rows = pl.ds(pl.multiple_of(m * 256, 256), 256)
            blocks = pl.ds(2 * m, 2)
            result = dot(h[rows], down_v[i]).astype(BF16)
            snd[2 * i, blocks] = result[:, :W].reshape(2, 128, W)
            snd[2 * i + 1, blocks] = result[:, W:].reshape(2, 128, W)
            return carry

        lax.fori_loop(0, 4, tile, 0)
        for half in (0, 1):
            c = 2 * i + half
            rcv[c, ey] = snd[c, ey]
            for s in (4, 3, 5, 2, 6, 1, 7):
                cross(c, s).start()

    def combine(i):
        loads(i)[1].wait()
        for half in (0, 1):
            c = 2 * i + half
            for s in range(1, 8):
                cross(c, s).wait_recv()

            def quad(q, carry):
                rows = rcv[c, :, pl.ds(pl.multiple_of(q * 32, 32), 32)].reshape(256, W)
                tokens = pl.ds(pl.multiple_of(q * 256, 256), 256)
                total = dot(comb[q], rows) + dot(hs[tokens], sd_v[i, :, half * W : half * W + W])
                part[c, q] = total.astype(BF16).reshape(4, 64, W)
                return carry

            lax.fori_loop(0, 4, quad, 0)
            for s in (2, 1, 3):
                first(c, half, s).start()

    def reduce(i):
        for half in (0, 1):
            c = 2 * i + half
            for s in (1, 2, 3):
                first(c, half, s).wait_recv()
            for b in range(4):
                mine = part[c, y, b] if half == 0 else part[c, b, x]
                total = mine.astype(F32)
                for s in range(3):
                    total += got1[c, s, b].astype(F32)
                half_sum[c, b] = total.astype(BF16)
            for s in (2, 1, 3):
                second(c, half, s).start()

    def final(i):
        for half in (0, 1):
            c = 2 * i + half
            for s in (1, 2, 3):
                second(c, half, s).wait_recv()
            total = half_sum[c, x if half == 0 else y].astype(F32)
            for s in range(3):
                total += got2[c, s].astype(F32)
            out[:, pl.ds(pl.multiple_of(c * W, W), W)] = total.astype(BF16)

    def step(i, carry):
        @pl.when(i < pairs)
        def _():
            down(i)

        @pl.when((i >= 1) & (i < pairs + 1))
        def _():
            combine(i - 1)

        @pl.when((i >= 2) & (i < pairs + 2))
        def _():
            reduce(i - 2)

        @pl.when(i >= 3)
        def _():
            final(i - 3)

        return carry

    lax.fori_loop(0, pairs + 3, step, 0)

    def drain(i, carry):
        for half in (0, 1):
            c = 2 * i + half
            for s in (1, 2, 3):
                first(c, half, s).wait_send()
                second(c, half, s).wait_send()
            for s in range(1, 8):
                cross(c, s).wait_send()
        return carry

    lax.fori_loop(0, pairs, drain, 0)


def shards(
    tokens, route_ids, route_weight, w_gate, w_up, w_down, shared_gate, shared_up, shared_down
):
    width = tokens.shape[1]
    pairs = width // (2 * W)
    n = 2 * pairs
    vmem = pl.BlockSpec(memory_space=pltpu.VMEM)
    hbm = pl.BlockSpec(memory_space=pl.ANY)
    dma = pltpu.SemaphoreType.DMA
    hidden, shared_hidden, comb = pl.pallas_call(
        functools.partial(dispatch_kernel, pairs),
        out_shape=(
            jax.ShapeDtypeStruct((1024, 1024), BF16),
            jax.ShapeDtypeStruct((1024, 128), BF16),
            jax.ShapeDtypeStruct((4, 256, 256), BF16),
        ),
        in_specs=[vmem] * 3 + [hbm] * 4,
        out_specs=(vmem, vmem, vmem),
        scratch_shapes=[
            pltpu.VMEM((n, 4, 4, 64, W), BF16),
            pltpu.VMEM((n, 8, 128, W), BF16),
            pltpu.VMEM((n, 8, 128, W), BF16),
            pltpu.VMEM((1024, 1024), F32),
            pltpu.VMEM((1024, 1024), F32),
            pltpu.VMEM((pairs, 2 * W, 1024), BF16),
            pltpu.VMEM((pairs, 2 * W, 1024), BF16),
            pltpu.VMEM((pairs, 2 * W, 256), BF16),
            pltpu.VMEM((64, 128), F32),
            pltpu.VMEM((4, 4, 64, 128), F32),
            pltpu.VMEM((4, 256, 256), BF16),
            pltpu.VMEM((1024, 256), F32),
            dma((4, pairs)),
            dma((3,)), dma((3,)), dma((3,)), dma((3,)),
            dma((n, 3)), dma((n, 3)), dma((n, 3)), dma((n, 3)), dma((n, 7)), dma((n, 7)),
        ],
        compiler_params=pltpu.CompilerParams(
            collective_id=0, has_side_effects=True, vmem_limit_bytes=60 * 2**20
        ),
        name="dispatch",
    )(tokens, route_ids, route_weight, w_gate, w_up, shared_gate, shared_up)
    return pl.pallas_call(
        functools.partial(return_kernel, pairs),
        out_shape=jax.ShapeDtypeStruct((64, width), BF16),
        in_specs=[vmem] * 3 + [hbm] * 2,
        out_specs=vmem,
        scratch_shapes=[
            pltpu.VMEM((pairs, 1024, 2 * W), BF16),
            pltpu.VMEM((pairs, 128, 2 * W), BF16),
            pltpu.VMEM((n, 8, 128, W), BF16),
            pltpu.VMEM((n, 8, 128, W), BF16),
            pltpu.VMEM((n, 4, 4, 64, W), BF16),
            pltpu.VMEM((n, 3, 4, 64, W), BF16),
            pltpu.VMEM((n, 4, 64, W), BF16),
            pltpu.VMEM((n, 3, 64, W), BF16),
            dma((2, pairs)),
            dma((n, 7)), dma((n, 7)), dma((n, 3)), dma((n, 3)), dma((n, 3)), dma((n, 3)),
        ],
        compiler_params=pltpu.CompilerParams(
            collective_id=1, has_side_effects=True, vmem_limit_bytes=60 * 2**20
        ),
        name="bring_back",
    )(hidden, shared_hidden, comb, w_down, shared_down)


def solution(mesh):
    in_specs = (
        P(("ex", "ey"), None),
        P(("ex", "ey"), None),
        P(("ex", "ey"), None),
        P(("ex", "ey"), None, None),
        P(("ex", "ey"), None, None),
        P(("ex", "ey"), None, None),
        P(None, "ex"),
        P(None, "ex"),
        P("ex", None),
    )
    out_specs = P(("ex", "ey"), None)
    return jax.shard_map(shards, mesh=mesh, in_specs=in_specs, out_specs=out_specs, check_vma=False)
```

```python
import functools

import jax
import jax.numpy as jnp
from jax import lax
from jax.experimental import pallas as pl
from jax.experimental.pallas import tpu as pltpu
from jax.sharding import PartitionSpec as P

MESH = pl.DeviceIdType.MESH
F32 = jnp.float32
BF16 = jnp.bfloat16
LAG = 2
W = 256


def dot(a, b):
    return jnp.dot(a, b, preferred_element_type=F32)


NEAR = ((0, 0), (0, 1), (1, 0), (1, 1), (3, 0), (3, 1))
FAR = tuple((dy, dc) for dy in range(4) for dc in range(2))


class Place:
    def __init__(self):
        self.ex = lax.axis_index("ex")
        self.ey = lax.axis_index("ey")
        self.x = lax.rem(self.ex, 4)
        self.y = lax.div(self.ex, 4)
        self.z = lax.div(self.ey, 2)
        self.c = lax.rem(self.ey, 2)

    def at(self, dx, dy, dz, dc):
        ex = lax.rem(self.y + dy, 4) * 4 + lax.rem(self.x + dx, 4)
        ey = lax.rem(self.z + dz, 4) * 2 + lax.rem(self.c + dc, 2)
        return (ex, ey)

    def along(self, axis, step):
        return self.at(step, 0, 0, 0) if axis == "x" else self.at(0, step, 0, 0)

    def greet(self):
        barrier = pltpu.get_barrier_semaphore()
        partners = [self.along(axis, s) for axis in ("x", "y") for s in (1, 2, 3)]
        partners += [self.at(0, 0, dz, dc) for dz, dc in NEAR[1:]]
        partners += [self.at(0, 0, 2, 0)]
        partners += [self.at(0, dy, 0, 1) for dy in (1, 2, 3)]
        for partner in partners:
            pl.semaphore_signal(barrier, inc=1, device_id=partner, device_id_type=MESH)
        pl.semaphore_wait(barrier, len(partners))


def remote(src, dst, send, recv, partner):
    return pltpu.make_async_remote_copy(
        src_ref=src, dst_ref=dst, send_sem=send, recv_sem=recv, device_id=partner, device_id_type=MESH
    )


def chunk(c):
    return pl.ds(pl.multiple_of(c * W, W), W)


def line(ref, c, axis, index, part=slice(0, 4)):
    if axis == "y":
        return ref.at[c, index, part]
    return ref.at[c, part, index]


def dispatch_kernel(
    pairs,
    tok, ids, weight, w_gate, w_up, s_gate, s_up,
    h_out, hs_out, comb, comb_far,
    ag, far, snd, rcv, snd_far, rcv_far, acc_g, acc_u, gate_v, up_v, sgu,
    meta, metas, metas_far, place_t, place_far, acc_s,
    load_sem, m_send, m_recv, p1_send, p1_recv, p2_send, p2_recv, fw_send, fw_recv,
    a_send, a_recv, f_send, f_recv, z_send, z_recv, y_send, y_recv,
):
    here = Place()
    x, y, z, core = here.x, here.y, here.z, here.c

    def load(i, which):
        rows = pl.ds(pl.multiple_of(i * 2 * W, 2 * W), 2 * W)
        src, dst = (
            (w_gate.at[0, rows], gate_v.at[i]),
            (w_up.at[0, rows], up_v.at[i]),
            (s_gate.at[rows], sgu.at[i, :, pl.ds(0, 128)]),
            (s_up.at[rows], sgu.at[i, :, pl.ds(128, 128)]),
        )[which]
        return pltpu.make_async_copy(src, dst, load_sem.at[which, i])

    def start_loads(i, carry):
        for which in range(4):
            load(i, which).start()
        return carry

    lane = lax.broadcasted_iota(jnp.int32, (64, 128), 1)
    hits = [ids[:, k : k + 1] == lane for k in range(8)]
    named = sum(jnp.where(hit, 1.0, 0.0) for hit in hits)
    lower = lax.broadcasted_iota(jnp.int32, (64, 64), 0) > lax.broadcasted_iota(jnp.int32, (64, 64), 1)
    before = dot(jnp.where(lower, 1.0, 0.0).astype(BF16), named.astype(BF16))
    info = jnp.zeros((64, 128), F32)
    for k in range(8):
        rank = jnp.sum(jnp.where(hits[k], before, 0.0), axis=1, keepdims=True)
        code = ids[:, k : k + 1].astype(F32) * 32.0 + rank
        info = jnp.where(lane == k, code, info)
        info = jnp.where(lane == 8 + k, weight[:, k : k + 1].astype(F32), info)
    meta[...] = info
    metas[y, x] = info

    def own(c, carry):
        ag[c, y, x] = tok[:, chunk(c)]
        return carry

    lax.fori_loop(0, 2 * pairs, own, 0)

    here.greet()

    def lead(half):
        return ("x", "y") if half == 0 else ("y", "x")

    def place(axis):
        return x if axis == "x" else y

    def first(c, half, s):
        partner = here.along(lead(half)[0], s)
        return remote(tok.at[:, chunk(c)], ag.at[c, y, x], p1_send.at[c, s - 1], p1_recv.at[c, s - 1], partner)

    def second(c, half, d):
        axis = lead(half)[1]
        block = line(ag, c, axis, place(axis))
        return remote(block, block, p2_send.at[c, d], p2_recv.at[c, d], here.along(axis, 1 + 2 * d))

    def onward(c, half, d):
        axis = lead(half)[1]
        origin = lax.rem(place(axis) + 3 - 2 * d, 4)
        block = line(ag, c, axis, origin, pl.ds(2 * d, 2))
        return remote(block, block, fw_send.at[c, d], fw_recv.at[c, d], here.along(axis, 1 + 2 * d))

    def opposite(c):
        return remote(tok.at[:, chunk(c)], far.at[c, x], a_send.at[c], a_recv.at[c], here.at(0, 0, 2, 0))

    def spread(c, s):
        return remote(far.at[c, x], far.at[c, x], f_send.at[c, s - 1], f_recv.at[c, s - 1], here.along("x", s))

    def near(c, b):
        dz, dc = NEAR[b]
        return remote(snd.at[c, b - 1], rcv.at[c, b], z_send.at[c, b - 1], z_recv.at[c, b - 1], here.at(0, 0, dz, dc))

    def near_far(c, j):
        dy, dc = FAR[j]
        return remote(
            snd_far.at[c, j - 1], rcv_far.at[c, j], y_send.at[c, j - 1], y_recv.at[c, j - 1], here.at(0, dy, 0, dc)
        )

    def meta_copy(stage, s):
        sems = m_send.at[stage, s - 1], m_recv.at[stage, s - 1]
        if stage == 0:
            return remote(meta, metas.at[y, x], *sems, here.along("x", s))
        if stage == 1:
            return remote(metas.at[y], metas.at[y], *sems, here.along("y", s))
        if stage == 2:
            return remote(meta, metas_far.at[x], *sems, here.at(0, 0, 2, 0))
        return remote(metas_far.at[x], metas_far.at[x], *sems, here.along("x", s))

    def start_first(i):
        for half in (0, 1):
            c = 2 * i + half
            for s in (2, 1, 3):
                first(c, half, s).start()
            opposite(c).start()

    def start_second(i):
        for half in (0, 1):
            c = 2 * i + half
            for s in (1, 2, 3):
                first(c, half, s).wait_recv()
            for d in (0, 1):
                second(c, half, d).start()
            opposite(c).wait_recv()
            for s in (2, 1, 3):
                spread(c, s).start()

    def start_onward(i):
        for half in (0, 1):
            c = 2 * i + half
            for d in (0, 1):
                second(c, half, d).wait_recv()
                onward(c, half, d).start()

    meta_copy(2, 1).start()
    for s in (2, 1, 3):
        meta_copy(0, s).start()
    start_first(0)
    start_first(1)
    for s in (1, 2, 3):
        meta_copy(0, s).wait_recv()
    for s in (2, 1, 3):
        meta_copy(1, s).start()
    meta_copy(2, 1).wait_recv()
    for s in (2, 1, 3):
        meta_copy(3, s).start()
    start_second(0)
    start_first(2)
    lax.fori_loop(0, pairs, start_loads, 0)

    def clear(r, carry):
        rows = pl.ds(pl.multiple_of(r * 64, 64), 64)
        acc_g[rows] = jnp.zeros((64, 1024), F32)
        acc_u[rows] = jnp.zeros((64, 1024), F32)
        acc_s[rows] = jnp.zeros((64, 256), F32)
        return carry

    start_second(1)
    start_onward(0)
    lax.fori_loop(0, 16, clear, 0)

    slot = lax.broadcasted_iota(jnp.int32, (8, 256), 1)[:1]
    group = lax.shift_right_logical(slot, 5)
    inner = lax.bitwise_and(slot, 7) + lax.bitwise_and(lax.shift_right_logical(slot, 3), 3) * 8192
    other = lax.bitwise_and(group + core, 1)
    outer = lax.shift_right_logical(group, 1)
    plane = lax.bitwise_and(z + outer + jnp.where(outer == 2, 1, 0), 3)
    want = jnp.where(outer == 3, -1, (here.ex * 8 + plane * 2 + other) * 32 + inner).astype(F32)
    row = lax.bitwise_and(y + outer, 3)
    want_far = ((row * 32 + x * 8 + z * 2 + other) * 32 + inner).astype(F32)
    source = lax.shift_right_logical(lax.broadcasted_iota(jnp.int32, (256, 128), 0), 6)[:, :1]
    shift = (source * 8192).astype(F32)

    def matrix(known, wanted):
        total = jnp.zeros((256, 256), F32)
        for k in range(8):
            hit = (known[:, k : k + 1] + shift) == wanted
            total = jnp.where(hit, known[:, 8 + k : 9 + k], total)
        return total.astype(BF16), jnp.where(total > 0.0, 1.0, 0.0).T.astype(BF16)

    for s in (1, 2, 3):
        meta_copy(1, s).wait_recv()

    def matrices(q, carry):
        comb[q], place_t[q] = matrix(metas[q].reshape(256, 128), want)
        return carry

    lax.fori_loop(0, 4, matrices, 0)
    for s in (1, 2, 3):
        meta_copy(3, s).wait_recv()
    comb_far[...], place_far[...] = matrix(metas_far[...].reshape(256, 128), want_far)

    def compact(i):
        for half in (0, 1):
            c = 2 * i + half
            for d in (0, 1):
                onward(c, half, d).wait_recv()

            for q in range(4):
                rows = dot(place_t[q, :192], ag[c, q].reshape(256, W)).astype(BF16).reshape(6, 32, W)
                span = slice(q * 32, q * 32 + 32)
                rcv[c, 0, span] = rows[0]
                snd[c, :, span] = rows[1:]
            for b in range(1, 6):
                near(c, b).start()
            for s in (1, 2, 3):
                spread(c, s).wait_recv()
            rows = dot(place_far[...], far[c].reshape(256, W)).astype(BF16).reshape(8, 32, W)
            rcv_far[c, 0] = rows[0]
            snd_far[c] = rows[1:]
            for j in (4, 5, 2, 3, 6, 7, 1):
                near_far(c, j).start()

    def shared(i):
        for which in (2, 3):
            load(i, which).wait()

        both = jnp.concatenate([ag[2 * i].reshape(1024, W), ag[2 * i + 1].reshape(1024, W)], axis=1)
        acc_s[...] += dot(both, sgu[i])

    def expert(i):
        for which in (0, 1):
            load(i, which).wait()
        for half in (0, 1):
            c = 2 * i + half
            for b in range(1, 6):
                near(c, b).wait_recv()
            for j in range(1, 8):
                near_far(c, j).wait_recv()

        def add(rows, left, right):
            both = jnp.concatenate([left, right], axis=1)
            acc_g[rows] += dot(both, gate_v[i])
            acc_u[rows] += dot(both, up_v[i])

        def tile(m, carry):
            blocks = pl.ds(2 * m, 2)
            add(
                pl.ds(pl.multiple_of(m * 256, 256), 256),
                rcv[2 * i, blocks].reshape(256, W),
                rcv[2 * i + 1, blocks].reshape(256, W),
            )
            return carry

        lax.fori_loop(0, 3, tile, 0)
        add(pl.ds(768, 256), rcv_far[2 * i].reshape(256, W), rcv_far[2 * i + 1].reshape(256, W))

    def step(i, carry):
        @pl.when(i + 3 < pairs)
        def _():
            start_first(i + 3)

        @pl.when(i + 2 < pairs)
        def _():
            start_second(i + 2)

        @pl.when(i + 1 < pairs)
        def _():
            start_onward(i + 1)

        @pl.when(i < pairs)
        def _():
            compact(i)
            shared(i)

        @pl.when(i >= LAG)
        def _():
            expert(i - LAG)

        return carry

    lax.fori_loop(0, pairs + LAG, step, 0)

    def finish(r, carry):
        rows = pl.ds(pl.multiple_of(r * 64, 64), 64)
        h_out[rows] = (jax.nn.silu(acc_g[rows]) * acc_u[rows]).astype(BF16)
        both = acc_s[rows]
        hs_out[rows] = (jax.nn.silu(both[:, :128]) * both[:, 128:]).astype(BF16)
        return carry

    lax.fori_loop(0, 16, finish, 0)

    for stage in (0, 1, 3):
        for s in (1, 2, 3):
            meta_copy(stage, s).wait_send()
    meta_copy(2, 1).wait_send()

    def drain(i, carry):
        for half in (0, 1):
            c = 2 * i + half
            for s in (1, 2, 3):
                first(c, half, s).wait_send()
                spread(c, s).wait_send()
            opposite(c).wait_send()
            for d in (0, 1):
                second(c, half, d).wait_send()
                onward(c, half, d).wait_send()
            for b in range(1, 6):
                near(c, b).wait_send()
            for j in range(1, 8):
                near_far(c, j).wait_send()
        return carry

    lax.fori_loop(0, pairs, drain, 0)


def return_kernel(
    pairs,
    h, hs, comb, comb_far, w_down, s_down,
    out,
    down_v, sd_v, snd, rcv, snd_far, rcv_far, part, relay, got1, half_sum, got2, part_far, got_far, sum_far, got_home,
    load_sem, z_send, z_recv, y_send, y_recv, r0_send, r0_recv, r1_send, r1_recv, r2_send, r2_recv,
    f_send, f_recv, a_send, a_recv,
):
    here = Place()
    x, y = here.x, here.y

    def load(i, which):
        columns = pl.ds(pl.multiple_of(i * 2 * W, 2 * W), 2 * W)
        src, dst = (
            (w_down.at[0, :, columns], down_v.at[i]),
            (s_down.at[:, columns], sd_v.at[i]),
        )[which]
        return pltpu.make_async_copy(src, dst, load_sem.at[which, i])

    def start_loads(i, carry):
        for which in (0, 1):
            load(i, which).start()
        return carry

    lax.fori_loop(0, pairs, start_loads, 0)
    here.greet()

    def lead(half):
        return ("y", "x") if half == 0 else ("x", "y")

    def place(axis, step=0):
        return lax.rem((x if axis == "x" else y) + step, 4)

    def near(c, b):
        dz, dc = NEAR[b]
        return remote(
            snd.at[c, b - 1], rcv.at[c, b], z_send.at[c, b - 1], z_recv.at[c, b - 1], here.at(0, 0, 4 - dz, dc)
        )

    def near_far(c, j):
        dy, dc = FAR[j]
        return remote(
            snd_far.at[c, j - 1], rcv_far.at[c, j], y_send.at[c, j - 1], y_recv.at[c, j - 1], here.at(0, 4 - dy, 0, dc)
        )

    def through(c, half, d):
        axis = lead(half)[0]
        block = line(part, c, axis, place(axis, 2), pl.ds(2 * d, 2))
        return remote(block, relay.at[c, d], r0_send.at[c, d], r0_recv.at[c, d], here.along(axis, 3 - 2 * d))

    def first(c, half, d):
        axis = lead(half)[0]
        block = line(part, c, axis, place(axis, 3 - 2 * d))
        return remote(block, got1.at[c, d], r1_send.at[c, d], r1_recv.at[c, d], here.along(axis, 3 - 2 * d))

    def second(c, half, s):
        axis = lead(half)[1]
        block = half_sum.at[c, place(axis, s)]
        return remote(block, got2.at[c, s - 1], r2_send.at[c, s - 1], r2_recv.at[c, s - 1], here.along(axis, s))

    def gather_far(c, s):
        block = part_far.at[c, place("x", s)]
        return remote(block, got_far.at[c, s - 1], f_send.at[c, s - 1], f_recv.at[c, s - 1], here.along("x", s))

    def home(c):
        return remote(sum_far.at[c], got_home.at[c], a_send.at[c], a_recv.at[c], here.at(0, 0, 2, 0))

    def down(i):
        load(i, 0).wait()
        for m in range(4):
            result = dot(h[m * 256 : m * 256 + 256], down_v[i]).astype(BF16)
            for half in (0, 1):
                c = 2 * i + half
                piece = result[:, half * W : half * W + W]
                if m == 3:
                    piece = piece.reshape(8, 32, W)
                    rcv_far[c, 0] = piece[0]
                    snd_far[c] = piece[1:]
                elif m == 0:
                    rcv[c, 0] = piece[:128]
                    snd[c, 0] = piece[128:]
                else:
                    snd[c, 2 * m - 1] = piece[:128]
                    snd[c, 2 * m] = piece[128:]
        for half in (0, 1):
            c = 2 * i + half
            for b in range(1, 6):
                near(c, b).start()
            for j in (4, 5, 2, 3, 6, 7, 1):
                near_far(c, j).start()

    def combine(i):
        load(i, 1).wait()
        for half in (0, 1):
            c = 2 * i + half
            for j in range(1, 8):
                near_far(c, j).wait_recv()
            total = dot(comb_far[...], rcv_far[c].reshape(256, W))
            part_far[c] = total.astype(BF16).reshape(4, 64, W)
            for b in range(1, 6):
                near(c, b).wait_recv()

            for q in range(4):
                rows = rcv[c, :, q * 32 : q * 32 + 32].reshape(192, W)
                rows = jnp.concatenate([sd_v[i, :, half * W : half * W + W], rows], axis=0)
                total = dot(jnp.concatenate([hs[q * 256 : q * 256 + 256], comb[q, :, :192]], axis=1), rows)
                part[c, q] = total.astype(BF16).reshape(4, 64, W)
            for d in (0, 1):
                through(c, half, d).start()
            for s in (2, 1, 3):
                gather_far(c, s).start()

    def pass_on(i):
        for half in (0, 1):
            c = 2 * i + half
            axis = lead(half)[0]
            for d in (0, 1):
                through(c, half, d).wait_recv()
                target = place(axis, 3 - 2 * d)
                for b in (2 * d, 2 * d + 1):
                    where = (c, target, b) if axis == "y" else (c, b, target)
                    part[where] = (part[where].astype(F32) + relay[c, d, b - 2 * d].astype(F32)).astype(BF16)
            for d in (0, 1):
                first(c, half, d).start()
            total = jnp.zeros((64, W), F32)
            for s in (1, 2, 3):
                gather_far(c, s).wait_recv()
                total += got_far[c, s - 1].astype(F32)
            sum_far[c] = (total + part_far[c, x].astype(F32)).astype(BF16)
            home(c).start()

    def reduce(i):
        for half in (0, 1):
            c = 2 * i + half
            for d in (0, 1):
                first(c, half, d).wait_recv()
            for b in range(4):
                mine = part[c, y, b] if half == 0 else part[c, b, x]
                total = mine.astype(F32) + got1[c, 0, b].astype(F32) + got1[c, 1, b].astype(F32)
                half_sum[c, b] = total.astype(BF16)
            for s in (2, 1, 3):
                second(c, half, s).start()

    def final(i):
        for half in (0, 1):
            c = 2 * i + half
            home(c).wait_recv()
            total = got_home[c].astype(F32) + half_sum[c, place(lead(half)[1])].astype(F32)
            for s in (1, 2, 3):
                second(c, half, s).wait_recv()
                total += got2[c, s - 1].astype(F32)
            out[:, chunk(c)] = total.astype(BF16)

    def step(i, carry):
        @pl.when(i < pairs)
        def _():
            down(i)

        @pl.when((i >= 2) & (i < pairs + 2))
        def _():
            pass_on(i - 2)

        @pl.when((i >= 3) & (i < pairs + 3))
        def _():
            reduce(i - 3)

        @pl.when(i >= 4)
        def _():
            final(i - 4)

        @pl.when((i >= 1) & (i < pairs + 1))
        def _():
            combine(i - 1)

        return carry

    lax.fori_loop(0, pairs + 4, step, 0)

    def drain(i, carry):
        for half in (0, 1):
            c = 2 * i + half
            for d in (0, 1):
                through(c, half, d).wait_send()
                first(c, half, d).wait_send()
            for s in (1, 2, 3):
                second(c, half, s).wait_send()
                gather_far(c, s).wait_send()
            home(c).wait_send()
            for b in range(1, 6):
                near(c, b).wait_send()
            for j in range(1, 8):
                near_far(c, j).wait_send()
        return carry

    lax.fori_loop(0, pairs, drain, 0)


def shards(
    tokens, route_ids, route_weight, w_gate, w_up, w_down, shared_gate, shared_up, shared_down
):
    width = tokens.shape[1]
    pairs = width // (2 * W)
    n = 2 * pairs
    vmem = pl.BlockSpec(memory_space=pltpu.VMEM)
    hbm = pl.BlockSpec(memory_space=pl.ANY)

    def both(*shape):
        return [pltpu.SemaphoreType.DMA(shape)] * 2

    def held(*shape, dtype=BF16):
        return pltpu.VMEM(shape, dtype)

    hidden, shared_hidden, comb, comb_far = pl.pallas_call(
        functools.partial(dispatch_kernel, pairs),
        out_shape=(
            jax.ShapeDtypeStruct((1024, 1024), BF16),
            jax.ShapeDtypeStruct((1024, 128), BF16),
            jax.ShapeDtypeStruct((4, 256, 256), BF16),
            jax.ShapeDtypeStruct((256, 256), BF16),
        ),
        in_specs=[vmem] * 3 + [hbm] * 4,
        out_specs=(vmem,) * 4,
        scratch_shapes=[
            held(n, 4, 4, 64, W),
            held(n, 4, 64, W),
            held(n, 5, 128, W),
            held(n, 6, 128, W),
            held(n, 7, 32, W),
            held(n, 8, 32, W),
            held(1024, 1024, dtype=F32),
            held(1024, 1024, dtype=F32),
            held(pairs, 2 * W, 1024),
            held(pairs, 2 * W, 1024),
            held(pairs, 2 * W, 256),
            held(64, 128, dtype=F32),
            held(4, 4, 64, 128, dtype=F32),
            held(4, 64, 128, dtype=F32),
            held(4, 256, 256),
            held(256, 256),
            held(1024, 256, dtype=F32),
            pltpu.SemaphoreType.DMA((4, pairs)),
            *both(4, 3), *both(n, 3), *both(n, 2), *both(n, 2),
            *both(n), *both(n, 3), *both(n, 5), *both(n, 7),
        ],
        compiler_params=pltpu.CompilerParams(
            collective_id=0, has_side_effects=True, vmem_limit_bytes=60 * 2**20
        ),
        name="dispatch",
    )(tokens, route_ids, route_weight, w_gate, w_up, shared_gate, shared_up)
    return pl.pallas_call(
        functools.partial(return_kernel, pairs),
        out_shape=jax.ShapeDtypeStruct((64, width), BF16),
        in_specs=[vmem] * 4 + [hbm] * 2,
        out_specs=vmem,
        scratch_shapes=[
            held(pairs, 1024, 2 * W),
            held(pairs, 128, 2 * W),
            held(n, 5, 128, W),
            held(n, 6, 128, W),
            held(n, 7, 32, W),
            held(n, 8, 32, W),
            held(n, 4, 4, 64, W),
            held(n, 2, 2, 64, W),
            held(n, 2, 4, 64, W),
            held(n, 4, 64, W),
            held(n, 3, 64, W),
            held(n, 4, 64, W),
            held(n, 3, 64, W),
            held(n, 64, W),
            held(n, 64, W),
            pltpu.SemaphoreType.DMA((2, pairs)),
            *both(n, 5), *both(n, 7), *both(n, 2), *both(n, 2), *both(n, 3), *both(n, 3), *both(n),
        ],
        compiler_params=pltpu.CompilerParams(
            collective_id=1, has_side_effects=True, vmem_limit_bytes=60 * 2**20
        ),
        name="bring_back",
    )(hidden, shared_hidden, comb, comb_far, w_down, shared_down)


def solution(mesh):
    in_specs = (
        P(("ex", "ey"), None),
        P(("ex", "ey"), None),
        P(("ex", "ey"), None),
        P(("ex", "ey"), None, None),
        P(("ex", "ey"), None, None),
        P(("ex", "ey"), None, None),
        P(None, "ex"),
        P(None, "ex"),
        P("ex", None),
    )
    out_specs = P(("ex", "ey"), None)
    return jax.shard_map(shards, mesh=mesh, in_specs=in_specs, out_specs=out_specs, check_vma=False)
```

```python
import functools

import jax
import jax.numpy as jnp
from jax import lax
from jax.experimental import pallas as pl
from jax.experimental.pallas import tpu as pltpu
from jax.sharding import PartitionSpec as P

MESH = pl.DeviceIdType.MESH
F32 = jnp.float32
BF16 = jnp.bfloat16
LAG = 1
FIRST, SECOND, ONWARD = 3, 2, 1
COMBINE, PASS, REDUCE, FINAL = 2, 5, 8, 11
STRAIGHT_BACK = 0
W = 256


def dot(a, b):
    return jnp.dot(a, b, preferred_element_type=F32)


NEAR = ((0, 0), (0, 1), (1, 0), (1, 1), (3, 0), (3, 1))
FAR = tuple((dy, dc) for dy in range(4) for dc in range(2))


class Place:
    def __init__(self):
        self.ex = lax.axis_index("ex")
        self.ey = lax.axis_index("ey")
        self.x = lax.rem(self.ex, 4)
        self.y = lax.div(self.ex, 4)
        self.z = lax.div(self.ey, 2)
        self.c = lax.rem(self.ey, 2)

    def at(self, dx, dy, dz, dc):
        ex = lax.rem(self.y + dy, 4) * 4 + lax.rem(self.x + dx, 4)
        ey = lax.rem(self.z + dz, 4) * 2 + lax.rem(self.c + dc, 2)
        return (ex, ey)

    def along(self, axis, step):
        return self.at(step, 0, 0, 0) if axis == "x" else self.at(0, step, 0, 0)

    def greet(self):
        barrier = pltpu.get_barrier_semaphore()
        partners = [self.along(axis, s) for axis in ("x", "y") for s in (1, 2, 3)]
        partners += [self.at(0, 0, dz, dc) for dz, dc in NEAR[1:]]
        partners += [self.at(0, 0, 2, 0)]
        partners += [self.at(0, dy, 0, 1) for dy in (1, 2, 3)]
        for partner in partners:
            pl.semaphore_signal(barrier, inc=1, device_id=partner, device_id_type=MESH)
        pl.semaphore_wait(barrier, len(partners))


def when(condition, action):
    if isinstance(condition, bool):
        if condition:
            action()
    else:
        pl.when(condition)(action)


def remote(src, dst, send, recv, partner):
    return pltpu.make_async_remote_copy(
        src_ref=src, dst_ref=dst, send_sem=send, recv_sem=recv, device_id=partner, device_id_type=MESH
    )


def chunk(c):
    return pl.ds(pl.multiple_of(c * W, W), W)


def line(ref, c, axis, index, part=slice(0, 4)):
    if axis == "y":
        return ref.at[c, index, part]
    return ref.at[c, part, index]


def dispatch_kernel(
    pairs,
    tok, ids, weight, w_gate, w_up, s_gate, s_up,
    h_out, hs_out, comb, comb_far,
    ag, far, snd, rcv, snd_far, rcv_far, acc_g, acc_u, gate_v, up_v, sgu,
    meta, metas, metas_far, place_t, place_far, acc_s,
    load_sem, m_send, m_recv, p1_send, p1_recv, p2_send, p2_recv, fw_send, fw_recv,
    a_send, a_recv, f_send, f_recv, z_send, z_recv, y_send, y_recv,
):
    here = Place()
    x, y, z, core = here.x, here.y, here.z, here.c

    def load(i, which):
        rows = pl.ds(pl.multiple_of(i * 2 * W, 2 * W), 2 * W)
        src, dst = (
            (w_gate.at[0, rows], gate_v.at[i]),
            (w_up.at[0, rows], up_v.at[i]),
            (s_gate.at[rows], sgu.at[i, :, pl.ds(0, 128)]),
            (s_up.at[rows], sgu.at[i, :, pl.ds(128, 128)]),
        )[which]
        return pltpu.make_async_copy(src, dst, load_sem.at[which, i])

    def start_loads(i, carry):
        for which in range(4):
            load(i, which).start()
        return carry

    here.greet()

    def lead(half):
        return ("x", "y") if half == 0 else ("y", "x")

    def place(axis):
        return x if axis == "x" else y

    def first(c, half, s):
        partner = here.along(lead(half)[0], s)
        return remote(tok.at[:, chunk(c)], ag.at[c, y, x], p1_send.at[c, s - 1], p1_recv.at[c, s - 1], partner)

    def second(c, half, d):
        axis = lead(half)[1]
        block = line(ag, c, axis, place(axis))
        return remote(block, block, p2_send.at[c, d], p2_recv.at[c, d], here.along(axis, 1 + 2 * d))

    def onward(c, half, d):
        axis = lead(half)[1]
        origin = lax.rem(place(axis) + 3 - 2 * d, 4)
        block = line(ag, c, axis, origin, pl.ds(2 * d, 2))
        return remote(block, block, fw_send.at[c, d], fw_recv.at[c, d], here.along(axis, 1 + 2 * d))

    def opposite(c):
        return remote(tok.at[:, chunk(c)], far.at[c, x], a_send.at[c], a_recv.at[c], here.at(0, 0, 2, 0))

    def spread(c, s):
        return remote(far.at[c, x], far.at[c, x], f_send.at[c, s - 1], f_recv.at[c, s - 1], here.along("x", s))

    def near(c, b):
        dz, dc = NEAR[b]
        return remote(snd.at[c, b - 1], rcv.at[c, b], z_send.at[c, b - 1], z_recv.at[c, b - 1], here.at(0, 0, dz, dc))

    def near_far(c, j):
        dy, dc = FAR[j]
        return remote(
            snd_far.at[c, j - 1], rcv_far.at[c, j], y_send.at[c, j - 1], y_recv.at[c, j - 1], here.at(0, dy, 0, dc)
        )

    def meta_copy(stage, s):
        sems = m_send.at[stage, s - 1], m_recv.at[stage, s - 1]
        if stage == 0:
            return remote(meta, metas.at[y, x], *sems, here.along("x", s))
        if stage == 1:
            return remote(metas.at[y], metas.at[y], *sems, here.along("y", s))
        if stage == 2:
            return remote(meta, metas_far.at[x], *sems, here.at(0, 0, 2, 0))
        return remote(metas_far.at[x], metas_far.at[x], *sems, here.along("x", s))

    def start_first(i):
        for half in (0, 1):
            c = 2 * i + half
            for s in (2, 1, 3):
                first(c, half, s).start()
            opposite(c).start()

    def start_second(i):
        for half in (0, 1):
            c = 2 * i + half
            for s in (1, 2, 3):
                first(c, half, s).wait_recv()
            for d in (0, 1):
                second(c, half, d).start()
            opposite(c).wait_recv()
            for s in (2, 1, 3):
                spread(c, s).start()

    def start_onward(i):
        for half in (0, 1):
            c = 2 * i + half
            for d in (0, 1):
                second(c, half, d).wait_recv()
                onward(c, half, d).start()

    def meta_of_slots():
        pad = jnp.zeros((64, 128), F32)
        turned_ids = jnp.concatenate([ids[...].astype(F32), jnp.zeros((120, 64), F32)], axis=0).T
        turned_weight = jnp.concatenate([weight[...].astype(F32), jnp.zeros((120, 64), F32)], axis=0).T
        lane = lax.broadcasted_iota(jnp.int32, (64, 128), 1)
        name = lane.astype(F32)
        hits = [turned_ids[:, k : k + 1] == name for k in range(8)]
        named = sum(jnp.where(hit, 1.0, 0.0) for hit in hits)
        lower = lax.broadcasted_iota(jnp.int32, (64, 64), 0) > lax.broadcasted_iota(jnp.int32, (64, 64), 1)
        before = dot(jnp.where(lower, 1.0, 0.0).astype(BF16), named.astype(BF16))
        info = pad
        for k in range(8):
            rank = jnp.sum(jnp.where(hits[k], before, 0.0), axis=1, keepdims=True)
            info = jnp.where(lane == k, turned_ids[:, k : k + 1] * 32.0 + rank, info)
            info = jnp.where(lane == 8 + k, turned_weight[:, k : k + 1], info)
        meta[...] = info
        metas[y, x] = info

    def own(c, carry):
        ag[c, y, x] = tok[:, chunk(c)]
        return carry

    def clear(r, carry):
        rows = pl.ds(pl.multiple_of(r * 64, 64), 64)
        acc_g[rows] = jnp.zeros((64, 1024), F32)
        acc_u[rows] = jnp.zeros((64, 1024), F32)
        acc_s[rows] = jnp.zeros((64, 256), F32)
        return carry

    start_first(0)
    lax.fori_loop(0, 2 * pairs, own, 0)
    meta_of_slots()
    meta_copy(2, 1).start()
    for s in (2, 1, 3):
        meta_copy(0, s).start()
    for i in range(1, FIRST):
        start_first(i)
        if i == 1:
            start_second(0)
        if i == 2:
            for s in (1, 2, 3):
                meta_copy(0, s).wait_recv()
            for s in (2, 1, 3):
                meta_copy(1, s).start()
            meta_copy(2, 1).wait_recv()
            for s in (2, 1, 3):
                meta_copy(3, s).start()
            lax.fori_loop(0, pairs, start_loads, 0)
    lax.fori_loop(0, 16, clear, 0)
    for i in range(1, SECOND):
        start_second(i)
        if i == 1:
            start_onward(0)
    for i in range(1, ONWARD):
        start_onward(i)

    slot = lax.broadcasted_iota(jnp.int32, (8, 256), 1)[:1]
    group = lax.shift_right_logical(slot, 5)
    inner = lax.bitwise_and(slot, 7) + lax.bitwise_and(lax.shift_right_logical(slot, 3), 3) * 8192
    other = lax.bitwise_and(group + core, 1)
    outer = lax.shift_right_logical(group, 1)
    plane = lax.bitwise_and(z + outer + jnp.where(outer == 2, 1, 0), 3)
    want = jnp.where(outer == 3, -1, (here.ex * 8 + plane * 2 + other) * 32 + inner).astype(F32)
    row = lax.bitwise_and(y + outer, 3)
    want_far = ((row * 32 + x * 8 + z * 2 + other) * 32 + inner).astype(F32)
    source = lax.shift_right_logical(lax.broadcasted_iota(jnp.int32, (256, 128), 0), 6)[:, :1]
    shift = (source * 8192).astype(F32)

    def matrix(known, wanted):
        total = jnp.zeros((256, 256), F32)
        for k in range(8):
            hit = (known[:, k : k + 1] + shift) == wanted
            total = jnp.where(hit, known[:, 8 + k : 9 + k], total)
        return total.astype(BF16), jnp.where(total > 0.0, 1.0, 0.0).T.astype(BF16)

    for s in (1, 2, 3):
        meta_copy(1, s).wait_recv()

    def matrices(q, carry):
        comb[q], place_t[q] = matrix(metas[q].reshape(256, 128), want)
        return carry

    lax.fori_loop(0, 4, matrices, 0)
    for s in (1, 2, 3):
        meta_copy(3, s).wait_recv()
    comb_far[...], place_far[...] = matrix(metas_far[...].reshape(256, 128), want_far)

    def compact(i):
        for half in (0, 1):
            c = 2 * i + half
            for d in (0, 1):
                onward(c, half, d).wait_recv()

            for q in range(4):
                rows = dot(place_t[q, :192], ag[c, q].reshape(256, W)).astype(BF16).reshape(6, 32, W)
                span = slice(q * 32, q * 32 + 32)
                rcv[c, 0, span] = rows[0]
                snd[c, :, span] = rows[1:]
            for b in range(1, 6):
                near(c, b).start()
            for s in (1, 2, 3):
                spread(c, s).wait_recv()
            rows = dot(place_far[...], far[c].reshape(256, W)).astype(BF16).reshape(8, 32, W)
            rcv_far[c, 0] = rows[0]
            snd_far[c] = rows[1:]
            for j in (4, 5, 2, 3, 6, 7, 1):
                near_far(c, j).start()

    def shared(i):
        for which in (2, 3):
            load(i, which).wait()

        both = jnp.concatenate([ag[2 * i].reshape(1024, W), ag[2 * i + 1].reshape(1024, W)], axis=1)
        acc_s[...] += dot(both, sgu[i])

    def expert(i):
        for which in (0, 1):
            load(i, which).wait()
        for half in (0, 1):
            c = 2 * i + half
            for b in range(1, 6):
                near(c, b).wait_recv()
            for j in range(1, 8):
                near_far(c, j).wait_recv()

        def add(rows, left, right):
            both = jnp.concatenate([left, right], axis=1)
            acc_g[rows] += dot(both, gate_v[i])
            acc_u[rows] += dot(both, up_v[i])

        def tile(m, carry):
            blocks = pl.ds(2 * m, 2)
            add(
                pl.ds(pl.multiple_of(m * 256, 256), 256),
                rcv[2 * i, blocks].reshape(256, W),
                rcv[2 * i + 1, blocks].reshape(256, W),
            )
            return carry

        lax.fori_loop(0, 3, tile, 0)
        add(pl.ds(768, 256), rcv_far[2 * i].reshape(256, W), rcv_far[2 * i + 1].reshape(256, W))

    def step(i, carry):
        @pl.when(i + FIRST < pairs)
        def _():
            start_first(i + FIRST)

        @pl.when(i + SECOND < pairs)
        def _():
            start_second(i + SECOND)

        @pl.when(i + ONWARD < pairs)
        def _():
            start_onward(i + ONWARD)

        @pl.when(i < pairs)
        def _():
            compact(i)
            shared(i)

        @pl.when(i >= LAG)
        def _():
            expert(i - LAG)

        return carry

    lax.fori_loop(0, pairs + LAG, step, 0)

    def finish(r, carry):
        rows = pl.ds(pl.multiple_of(r * 64, 64), 64)
        h_out[rows] = (jax.nn.silu(acc_g[rows]) * acc_u[rows]).astype(BF16)
        both = acc_s[rows]
        hs_out[rows] = (jax.nn.silu(both[:, :128]) * both[:, 128:]).astype(BF16)
        return carry

    lax.fori_loop(0, 16, finish, 0)

    for stage in (0, 1, 3):
        for s in (1, 2, 3):
            meta_copy(stage, s).wait_send()
    meta_copy(2, 1).wait_send()

    def drain(i, carry):
        for half in (0, 1):
            c = 2 * i + half
            for s in (1, 2, 3):
                first(c, half, s).wait_send()
                spread(c, s).wait_send()
            opposite(c).wait_send()
            for d in (0, 1):
                second(c, half, d).wait_send()
                onward(c, half, d).wait_send()
            for b in range(1, 6):
                near(c, b).wait_send()
            for j in range(1, 8):
                near_far(c, j).wait_send()
        return carry

    lax.fori_loop(0, pairs, drain, 0)


def return_kernel(
    pairs,
    h, hs, comb, comb_far, w_down, s_down,
    out,
    down_v, sd_v, snd, rcv, rcv_two, snd_far, rcv_far, part, relay, got1, half_sum, got2, part_far, relay_far, got_far, sum_far, got_home,
    load_sem, z_send, z_recv, y_send, y_recv, r0_send, r0_recv, r1_send, r1_recv, r2_send, r2_recv,
    f_send, f_recv, g_send, g_recv, a_send, a_recv,
):
    here = Place()
    x, y = here.x, here.y
    n = 2 * pairs

    def load(i, which):
        columns = pl.ds(pl.multiple_of(i * 2 * W, 2 * W), 2 * W)
        src, dst = (
            (w_down.at[0, :, columns], down_v.at[i]),
            (s_down.at[:, columns], sd_v.at[i]),
        )[which]
        return pltpu.make_async_copy(src, dst, load_sem.at[which, i])

    def start_loads(i, carry):
        for which in (0, 1):
            load(i, which).start()
        return carry

    lax.fori_loop(0, pairs, start_loads, 0)
    here.greet()

    def lead(half):
        return ("y", "x") if half == 0 else ("x", "y")

    def place(axis, step=0):
        return lax.rem((x if axis == "x" else y) + step, 4)

    def near(c, b):
        dz, dc = NEAR[b]
        return remote(
            snd.at[c, b - 1], rcv.at[c, b], z_send.at[c, b - 1], z_recv.at[c, b - 1], here.at(0, 0, 4 - dz, dc)
        )

    def near_far(c, j):
        dy, dc = FAR[j]
        return remote(
            snd_far.at[c, j], rcv_far.at[c, j], y_send.at[c, j], y_recv.at[c, j], here.at(0, 4 - dy, 0, dc)
        )

    def near_two(c, j):
        dy, dc = FAR[j]
        rows = pl.ds(pl.multiple_of(lax.rem(y + 4 - dy, 4) * 32, 32), 32)
        return remote(
            snd_far.at[c, j], rcv_two.at[c, dc, rows], y_send.at[c, j], y_recv.at[c, j], here.at(0, 0, 2, dc)
        )

    def far_rows(c, what):
        def straight():
            for j in range(8):
                getattr(near_two(c, j), what)()

        def around():
            for j in (4, 5, 2, 3, 6, 7, 1):
                getattr(near_far(c, j), what)()

        when(c >= n - STRAIGHT_BACK, straight)
        when(c < n - STRAIGHT_BACK, around)

    def through(c, half, d):
        axis = lead(half)[0]
        block = line(part, c, axis, place(axis, 2), pl.ds(2 * d, 2))
        return remote(block, relay.at[c, d], r0_send.at[c, d], r0_recv.at[c, d], here.along(axis, 3 - 2 * d))

    def first(c, half, d):
        axis = lead(half)[0]
        block = line(part, c, axis, place(axis, 3 - 2 * d))
        return remote(block, got1.at[c, d], r1_send.at[c, d], r1_recv.at[c, d], here.along(axis, 3 - 2 * d))

    def second(c, half, s):
        axis = lead(half)[1]
        block = half_sum.at[c, place(axis, s)]
        return remote(block, got2.at[c, s - 1], r2_send.at[c, s - 1], r2_recv.at[c, s - 1], here.along(axis, s))

    def through_far(c, d):
        block = part_far.at[c, place("x", 2), pl.ds(32 * d, 32)]
        return remote(block, relay_far.at[c, d], g_send.at[c, d], g_recv.at[c, d], here.along("x", 3 - 2 * d))

    def gather_far(c, d):
        block = part_far.at[c, place("x", 3 - 2 * d)]
        return remote(block, got_far.at[c, d], f_send.at[c, d], f_recv.at[c, d], here.along("x", 3 - 2 * d))

    def home(c):
        return remote(sum_far.at[c], got_home.at[c], a_send.at[c], a_recv.at[c], here.at(0, 0, 2, 0))

    def down(c, half):
        i = lax.div(c, 2)
        if half == 0:
            load(i, 0).wait()
        for m in range(4):
            piece = dot(h[m * 256 : m * 256 + 256], down_v[i, :, half * W : half * W + W]).astype(BF16)
            if m == 3:
                piece = piece.reshape(8, 32, W)
                rcv_far[c, 0] = piece[0]
                snd_far[c] = piece
            elif m == 0:
                rcv[c, 0] = piece[:128]
                snd[c, 0] = piece[128:]
            else:
                snd[c, 2 * m - 1] = piece[:128]
                snd[c, 2 * m] = piece[128:]
        for b in range(1, 6):
            near(c, b).start()
        far_rows(c, "start")

    def combine(c, half):
        i = lax.div(c, 2)
        if half == 0:
            load(i, 1).wait()
        far_rows(c, "wait_recv")

        def far_part():
            total = dot(comb_far[...], rcv_far[c].reshape(256, W))
            part_far[c] = total.astype(BF16).reshape(4, 64, W)
            for d in (0, 1):
                through_far(c, d).start()

        def near_part(count):
            for q in range(4):
                span = slice(q * 32, q * 32 + 32)
                rows = [sd_v[i, :, half * W : half * W + W], rcv[c, :, span].reshape(192, W)]
                if count == 8:
                    rows.append(rcv_two[c, :, span].reshape(64, W))
                left = jnp.concatenate([hs[q * 256 : q * 256 + 256], comb[q, :, : count * 32]], axis=1)
                part[c, q] = dot(left, jnp.concatenate(rows, axis=0)).astype(BF16).reshape(4, 64, W)

        when(c < n - STRAIGHT_BACK, far_part)
        for b in range(1, 6):
            near(c, b).wait_recv()
        when(c < n - STRAIGHT_BACK, lambda: near_part(6))
        when(c >= n - STRAIGHT_BACK, lambda: near_part(8))
        for d in (0, 1):
            through(c, half, d).start()

    def pass_on(c, half):
        axis = lead(half)[0]
        for d in (0, 1):
            through(c, half, d).wait_recv()
            target = place(axis, 3 - 2 * d)
            for b in (2 * d, 2 * d + 1):
                where = (c, target, b) if axis == "y" else (c, b, target)
                part[where] = (part[where].astype(F32) + relay[c, d, b - 2 * d].astype(F32)).astype(BF16)
        for d in (0, 1):
            first(c, half, d).start()

        def go():
            for d in (0, 1):
                through_far(c, d).wait_recv()
                where = (c, place("x", 3 - 2 * d), slice(32 * d, 32 * d + 32))
                part_far[where] = (part_far[where].astype(F32) + relay_far[c, d].astype(F32)).astype(BF16)
            for d in (0, 1):
                gather_far(c, d).start()

        when(c < n - STRAIGHT_BACK, go)

    def reduce(c, half):
        for d in (0, 1):
            first(c, half, d).wait_recv()
        for b in range(4):
            mine = part[c, y, b] if half == 0 else part[c, b, x]
            total = mine.astype(F32) + got1[c, 0, b].astype(F32) + got1[c, 1, b].astype(F32)
            half_sum[c, b] = total.astype(BF16)
        for s in (2, 1, 3):
            second(c, half, s).start()

        def send_home():
            total = part_far[c, x].astype(F32)
            for d in (0, 1):
                gather_far(c, d).wait_recv()
                total += got_far[c, d].astype(F32)
            sum_far[c] = total.astype(BF16)
            home(c).start()

        when(c < n - STRAIGHT_BACK, send_home)

    def final(c, half):
        total = half_sum[c, place(lead(half)[1])].astype(F32)
        for s in (1, 2, 3):
            second(c, half, s).wait_recv()
            total += got2[c, s - 1].astype(F32)

        def with_far():
            home(c).wait_recv()
            out[:, chunk(c)] = (total + got_home[c].astype(F32)).astype(BF16)

        def without():
            out[:, chunk(c)] = total.astype(BF16)

        when(c < n - STRAIGHT_BACK, with_far)
        when(c >= n - STRAIGHT_BACK, without)

    def step(i, carry):
        for half in (0, 1):
            c = 2 * i + half
            for stage, lag in ((down, 0), (pass_on, PASS), (reduce, REDUCE), (final, FINAL), (combine, COMBINE)):

                @pl.when((c >= lag) & (c < n + lag))
                def _():
                    stage(c - lag, (half + lag) % 2)

        return carry

    lax.fori_loop(0, pairs + (FINAL + 1) // 2, step, 0)

    def drain(i, carry):
        for half in (0, 1):
            c = 2 * i + half
            for d in (0, 1):
                through(c, half, d).wait_send()
                first(c, half, d).wait_send()
            for s in (1, 2, 3):
                second(c, half, s).wait_send()

            def sent():
                for d in (0, 1):
                    through_far(c, d).wait_send()
                    gather_far(c, d).wait_send()
                home(c).wait_send()

            when(c < n - STRAIGHT_BACK, sent)
            for b in range(1, 6):
                near(c, b).wait_send()
            far_rows(c, "wait_send")
        return carry

    lax.fori_loop(0, pairs, drain, 0)


def shards(
    tokens, route_ids, route_weight, w_gate, w_up, w_down, shared_gate, shared_up, shared_down
):
    width = tokens.shape[1]
    pairs = width // (2 * W)
    n = 2 * pairs
    vmem = pl.BlockSpec(memory_space=pltpu.VMEM)
    hbm = pl.BlockSpec(memory_space=pl.ANY)

    def both(*shape):
        return [pltpu.SemaphoreType.DMA(shape)] * 2

    def held(*shape, dtype=BF16):
        return pltpu.VMEM(shape, dtype)

    hidden, shared_hidden, comb, comb_far = pl.pallas_call(
        functools.partial(dispatch_kernel, pairs),
        out_shape=(
            jax.ShapeDtypeStruct((1024, 1024), BF16),
            jax.ShapeDtypeStruct((1024, 128), BF16),
            jax.ShapeDtypeStruct((4, 256, 256), BF16),
            jax.ShapeDtypeStruct((256, 256), BF16),
        ),
        in_specs=[vmem] * 3 + [hbm] * 4,
        out_specs=(vmem,) * 4,
        scratch_shapes=[
            held(n, 4, 4, 64, W),
            held(n, 4, 64, W),
            held(n, 5, 128, W),
            held(n, 6, 128, W),
            held(n, 7, 32, W),
            held(n, 8, 32, W),
            held(1024, 1024, dtype=F32),
            held(1024, 1024, dtype=F32),
            held(pairs, 2 * W, 1024),
            held(pairs, 2 * W, 1024),
            held(pairs, 2 * W, 256),
            held(64, 128, dtype=F32),
            held(4, 4, 64, 128, dtype=F32),
            held(4, 64, 128, dtype=F32),
            held(4, 256, 256),
            held(256, 256),
            held(1024, 256, dtype=F32),
            pltpu.SemaphoreType.DMA((4, pairs)),
            *both(4, 3), *both(n, 3), *both(n, 2), *both(n, 2),
            *both(n), *both(n, 3), *both(n, 5), *both(n, 7),
        ],
        compiler_params=pltpu.CompilerParams(
            collective_id=0, has_side_effects=True, vmem_limit_bytes=60 * 2**20
        ),
        name="dispatch",
    )(tokens, route_ids.T, route_weight.T, w_gate, w_up, shared_gate, shared_up)
    return pl.pallas_call(
        functools.partial(return_kernel, pairs),
        out_shape=jax.ShapeDtypeStruct((64, width), BF16),
        in_specs=[vmem] * 4 + [hbm] * 2,
        out_specs=vmem,
        scratch_shapes=[
            held(pairs, 1024, 2 * W),
            held(pairs, 128, 2 * W),
            held(n, 5, 128, W),
            held(n, 6, 128, W),
            held(n, 2, 128, W),
            held(n, 8, 32, W),
            held(n, 8, 32, W),
            held(n, 4, 4, 64, W),
            held(n, 2, 2, 64, W),
            held(n, 2, 4, 64, W),
            held(n, 4, 64, W),
            held(n, 3, 64, W),
            held(n, 4, 64, W),
            held(n, 2, 32, W),
            held(n, 2, 64, W),
            held(n, 64, W),
            held(n, 64, W),
            pltpu.SemaphoreType.DMA((2, pairs)),
            *both(n, 5), *both(n, 8), *both(n, 2), *both(n, 2), *both(n, 3),
            *both(n, 2), *both(n, 2), *both(n),
        ],
        compiler_params=pltpu.CompilerParams(
            collective_id=1, has_side_effects=True, vmem_limit_bytes=60 * 2**20
        ),
        name="bring_back",
    )(hidden, shared_hidden, comb, comb_far, w_down, shared_down)


def solution(mesh):
    in_specs = (
        P(("ex", "ey"), None),
        P(("ex", "ey"), None),
        P(("ex", "ey"), None),
        P(("ex", "ey"), None, None),
        P(("ex", "ey"), None, None),
        P(("ex", "ey"), None, None),
        P(None, "ex"),
        P(None, "ex"),
        P("ex", None),
    )
    out_specs = P(("ex", "ey"), None)
    return jax.shard_map(shards, mesh=mesh, in_specs=in_specs, out_specs=out_specs, check_vma=False)
```

```python
import functools

import jax
import jax.numpy as jnp
from jax import lax
from jax.experimental import pallas as pl
from jax.experimental.pallas import tpu as pltpu
from jax.sharding import PartitionSpec as P

MESH = pl.DeviceIdType.MESH
F32 = jnp.float32
BF16 = jnp.bfloat16
LAG = 1
FIRST, SECOND, ONWARD = 3, 2, 1
COMBINE, PASS, REDUCE, FINAL = 2, 5, 8, 11
STRAIGHT_BACK = 0
W = 256


def dot(a, b):
    return jnp.dot(a, b, preferred_element_type=F32)


NEAR = ((0, 0), (0, 1), (1, 0), (1, 1), (3, 0), (3, 1))
FAR = tuple((dy, dc) for dy in range(4) for dc in range(2))


class Place:
    def __init__(self):
        self.ex = lax.axis_index("ex")
        self.ey = lax.axis_index("ey")
        self.x = lax.rem(self.ex, 4)
        self.y = lax.div(self.ex, 4)
        self.z = lax.div(self.ey, 2)
        self.c = lax.rem(self.ey, 2)

    def at(self, dx, dy, dz, dc):
        ex = lax.rem(self.y + dy, 4) * 4 + lax.rem(self.x + dx, 4)
        ey = lax.rem(self.z + dz, 4) * 2 + lax.rem(self.c + dc, 2)
        return (ex, ey)

    def along(self, axis, step):
        return self.at(step, 0, 0, 0) if axis == "x" else self.at(0, step, 0, 0)

    def greet(self):
        barrier = pltpu.get_barrier_semaphore()
        partners = [self.along(axis, s) for axis in ("x", "y") for s in (1, 2, 3)]
        partners += [self.at(0, 0, dz, dc) for dz, dc in NEAR[1:]]
        partners += [self.at(0, 0, 2, 0)]
        partners += [self.at(0, dy, 0, 1) for dy in (1, 2, 3)]
        for partner in partners:
            pl.semaphore_signal(barrier, inc=1, device_id=partner, device_id_type=MESH)
        pl.semaphore_wait(barrier, len(partners))


def when(condition, action):
    if isinstance(condition, bool):
        if condition:
            action()
    else:
        pl.when(condition)(action)


def remote(src, dst, send, recv, partner):
    return pltpu.make_async_remote_copy(
        src_ref=src, dst_ref=dst, send_sem=send, recv_sem=recv, device_id=partner, device_id_type=MESH
    )


def chunk(c):
    return pl.ds(pl.multiple_of(c * W, W), W)


def line(ref, c, axis, index, part=slice(0, 4)):
    if axis == "y":
        return ref.at[c, index, part]
    return ref.at[c, part, index]


def dispatch_kernel(
    pairs,
    tok, ids, weight, w_gate, w_up, s_gate, s_up,
    h_out, hs_out, comb, comb_far,
    ag, far, snd, rcv, snd_far, rcv_far, acc_g, acc_u, gate_v, up_v, sgu,
    meta, metas, metas_far, place_t, place_far, acc_s,
    load_sem, m_send, m_recv, p1_send, p1_recv, p2_send, p2_recv, fw_send, fw_recv,
    a_send, a_recv, f_send, f_recv, g_send, g_recv, z_send, z_recv, y_send, y_recv,
):
    here = Place()
    x, y, z, core = here.x, here.y, here.z, here.c

    def load(i, which):
        rows = pl.ds(pl.multiple_of(i * 2 * W, 2 * W), 2 * W)
        src, dst = (
            (w_gate.at[0, rows], gate_v.at[i]),
            (w_up.at[0, rows], up_v.at[i]),
            (s_gate.at[rows], sgu.at[i, :, pl.ds(0, 128)]),
            (s_up.at[rows], sgu.at[i, :, pl.ds(128, 128)]),
        )[which]
        return pltpu.make_async_copy(src, dst, load_sem.at[which, i])

    def start_loads(i, carry):
        for which in range(4):
            load(i, which).start()
        return carry

    here.greet()

    def lead(half):
        return ("x", "y") if half == 0 else ("y", "x")

    def place(axis):
        return x if axis == "x" else y

    def first(c, half, s):
        partner = here.along(lead(half)[0], s)
        return remote(tok.at[:, chunk(c)], ag.at[c, y, x], p1_send.at[c, s - 1], p1_recv.at[c, s - 1], partner)

    def second(c, half, d):
        axis = lead(half)[1]
        block = line(ag, c, axis, place(axis))
        return remote(block, block, p2_send.at[c, d], p2_recv.at[c, d], here.along(axis, 1 + 2 * d))

    def onward(c, half, d):
        axis = lead(half)[1]
        origin = lax.rem(place(axis) + 3 - 2 * d, 4)
        block = line(ag, c, axis, origin, pl.ds(2 * d, 2))
        return remote(block, block, fw_send.at[c, d], fw_recv.at[c, d], here.along(axis, 1 + 2 * d))

    def opposite(c):
        return remote(tok.at[:, chunk(c)], far.at[c, x], a_send.at[c], a_recv.at[c], here.at(0, 0, 2, 0))

    def spread(c, d):
        return remote(far.at[c, x], far.at[c, x], f_send.at[c, d], f_recv.at[c, d], here.along("x", 1 + 2 * d))

    def spread_on(c, d):
        block = far.at[c, lax.rem(x + 3 - 2 * d, 4), pl.ds(32 * d, 32)]
        return remote(block, block, g_send.at[c, d], g_recv.at[c, d], here.along("x", 1 + 2 * d))

    def near(c, b):
        dz, dc = NEAR[b]
        return remote(snd.at[c, b - 1], rcv.at[c, b], z_send.at[c, b - 1], z_recv.at[c, b - 1], here.at(0, 0, dz, dc))

    def near_far(c, j):
        dy, dc = FAR[j]
        return remote(
            snd_far.at[c, j - 1], rcv_far.at[c, j], y_send.at[c, j - 1], y_recv.at[c, j - 1], here.at(0, dy, 0, dc)
        )

    def meta_copy(stage, s):
        sems = m_send.at[stage, s - 1], m_recv.at[stage, s - 1]
        if stage == 0:
            return remote(meta, metas.at[y, x], *sems, here.along("x", s))
        if stage == 1:
            return remote(metas.at[y], metas.at[y], *sems, here.along("y", s))
        if stage == 2:
            return remote(meta, metas_far.at[x], *sems, here.at(0, 0, 2, 0))
        return remote(metas_far.at[x], metas_far.at[x], *sems, here.along("x", s))

    def start_first(i):
        for half in (0, 1):
            c = 2 * i + half
            for s in (2, 1, 3):
                first(c, half, s).start()

    def start_second(i):
        for half in (0, 1):
            c = 2 * i + half
            for s in (1, 2, 3):
                first(c, half, s).wait_recv()
            for d in (0, 1):
                second(c, half, d).start()
            opposite(c).wait_recv()
            for d in (0, 1):
                spread(c, d).start()

    def start_onward(i):
        for half in (0, 1):
            c = 2 * i + half
            for d in (0, 1):
                second(c, half, d).wait_recv()
                onward(c, half, d).start()
            for d in (0, 1):
                spread(c, d).wait_recv()
                spread_on(c, d).start()

    def meta_of_slots():
        pad = jnp.zeros((64, 128), F32)
        turned_ids = jnp.concatenate([ids[...].astype(F32), jnp.zeros((120, 64), F32)], axis=0).T
        turned_weight = jnp.concatenate([weight[...].astype(F32), jnp.zeros((120, 64), F32)], axis=0).T
        lane = lax.broadcasted_iota(jnp.int32, (64, 128), 1)
        name = lane.astype(F32)
        hits = [turned_ids[:, k : k + 1] == name for k in range(8)]
        named = sum(jnp.where(hit, 1.0, 0.0) for hit in hits)
        lower = lax.broadcasted_iota(jnp.int32, (64, 64), 0) > lax.broadcasted_iota(jnp.int32, (64, 64), 1)
        before = dot(jnp.where(lower, 1.0, 0.0).astype(BF16), named.astype(BF16))
        info = pad
        for k in range(8):
            rank = jnp.sum(jnp.where(hits[k], before, 0.0), axis=1, keepdims=True)
            info = jnp.where(lane == k, turned_ids[:, k : k + 1] * 32.0 + rank, info)
            info = jnp.where(lane == 8 + k, turned_weight[:, k : k + 1], info)
        meta[...] = info
        metas[y, x] = info

    def own(c, carry):
        ag[c, y, x] = tok[:, chunk(c)]
        return carry

    def clear(r, carry):
        rows = pl.ds(pl.multiple_of(r * 64, 64), 64)
        acc_g[rows] = jnp.zeros((64, 1024), F32)
        acc_u[rows] = jnp.zeros((64, 1024), F32)
        acc_s[rows] = jnp.zeros((64, 256), F32)
        return carry

    def start_opposite(c, carry):
        opposite(c).start()
        return carry

    start_first(0)
    lax.fori_loop(0, 2 * pairs, start_opposite, 0)
    lax.fori_loop(0, 2 * pairs, own, 0)
    meta_of_slots()
    meta_copy(2, 1).start()
    for s in (2, 1, 3):
        meta_copy(0, s).start()
    for i in range(1, FIRST):
        start_first(i)
        if i == 1:
            start_second(0)
        if i == 2:
            for s in (1, 2, 3):
                meta_copy(0, s).wait_recv()
            for s in (2, 1, 3):
                meta_copy(1, s).start()
            meta_copy(2, 1).wait_recv()
            for s in (2, 1, 3):
                meta_copy(3, s).start()
            lax.fori_loop(0, pairs, start_loads, 0)
    lax.fori_loop(0, 16, clear, 0)
    for i in range(1, SECOND):
        start_second(i)
        if i == 1:
            start_onward(0)
    for i in range(1, ONWARD):
        start_onward(i)

    slot = lax.broadcasted_iota(jnp.int32, (8, 256), 1)[:1]
    group = lax.shift_right_logical(slot, 5)
    inner = lax.bitwise_and(slot, 7) + lax.bitwise_and(lax.shift_right_logical(slot, 3), 3) * 8192
    other = lax.bitwise_and(group + core, 1)
    outer = lax.shift_right_logical(group, 1)
    plane = lax.bitwise_and(z + outer + jnp.where(outer == 2, 1, 0), 3)
    want = jnp.where(outer == 3, -1, (here.ex * 8 + plane * 2 + other) * 32 + inner).astype(F32)
    row = lax.bitwise_and(y + outer, 3)
    want_far = ((row * 32 + x * 8 + z * 2 + other) * 32 + inner).astype(F32)
    source = lax.shift_right_logical(lax.broadcasted_iota(jnp.int32, (256, 128), 0), 6)[:, :1]
    shift = (source * 8192).astype(F32)

    def matrix(known, wanted):
        total = jnp.zeros((256, 256), F32)
        for k in range(8):
            hit = (known[:, k : k + 1] + shift) == wanted
            total = jnp.where(hit, known[:, 8 + k : 9 + k], total)
        return total.astype(BF16), jnp.where(total > 0.0, 1.0, 0.0).T.astype(BF16)

    for s in (1, 2, 3):
        meta_copy(1, s).wait_recv()

    def matrices(q, carry):
        comb[q], place_t[q] = matrix(metas[q].reshape(256, 128), want)
        return carry

    lax.fori_loop(0, 4, matrices, 0)
    for s in (1, 2, 3):
        meta_copy(3, s).wait_recv()
    comb_far[...], place_far[...] = matrix(metas_far[...].reshape(256, 128), want_far)

    def compact(i):
        for half in (0, 1):
            c = 2 * i + half
            for d in (0, 1):
                onward(c, half, d).wait_recv()

            for q in range(4):
                rows = dot(place_t[q, :192], ag[c, q].reshape(256, W)).astype(BF16).reshape(6, 32, W)
                span = slice(q * 32, q * 32 + 32)
                rcv[c, 0, span] = rows[0]
                snd[c, :, span] = rows[1:]
            for b in range(1, 6):
                near(c, b).start()
            for d in (0, 1):
                spread_on(c, d).wait_recv()
            rows = dot(place_far[...], far[c].reshape(256, W)).astype(BF16).reshape(8, 32, W)
            rcv_far[c, 0] = rows[0]
            snd_far[c] = rows[1:]
            for j in (4, 5, 2, 3, 6, 7, 1):
                near_far(c, j).start()

    def shared(i):
        for which in (2, 3):
            load(i, which).wait()

        both = jnp.concatenate([ag[2 * i].reshape(1024, W), ag[2 * i + 1].reshape(1024, W)], axis=1)
        acc_s[...] += dot(both, sgu[i])

    def expert(i):
        for which in (0, 1):
            load(i, which).wait()
        for half in (0, 1):
            c = 2 * i + half
            for b in range(1, 6):
                near(c, b).wait_recv()
            for j in range(1, 8):
                near_far(c, j).wait_recv()

        def add(rows, left, right):
            both = jnp.concatenate([left, right], axis=1)
            acc_g[rows] += dot(both, gate_v[i])
            acc_u[rows] += dot(both, up_v[i])

        def tile(m, carry):
            blocks = pl.ds(2 * m, 2)
            add(
                pl.ds(pl.multiple_of(m * 256, 256), 256),
                rcv[2 * i, blocks].reshape(256, W),
                rcv[2 * i + 1, blocks].reshape(256, W),
            )
            return carry

        lax.fori_loop(0, 3, tile, 0)
        add(pl.ds(768, 256), rcv_far[2 * i].reshape(256, W), rcv_far[2 * i + 1].reshape(256, W))

    def step(i, carry):
        @pl.when(i + FIRST < pairs)
        def _():
            start_first(i + FIRST)

        @pl.when(i + SECOND < pairs)
        def _():
            start_second(i + SECOND)

        @pl.when(i + ONWARD < pairs)
        def _():
            start_onward(i + ONWARD)

        @pl.when(i < pairs)
        def _():
            compact(i)
            shared(i)

        @pl.when(i >= LAG)
        def _():
            expert(i - LAG)

        return carry

    lax.fori_loop(0, pairs + LAG, step, 0)

    def finish(r, carry):
        rows = pl.ds(pl.multiple_of(r * 64, 64), 64)
        h_out[rows] = (jax.nn.silu(acc_g[rows]) * acc_u[rows]).astype(BF16)
        both = acc_s[rows]
        hs_out[rows] = (jax.nn.silu(both[:, :128]) * both[:, 128:]).astype(BF16)
        return carry

    lax.fori_loop(0, 16, finish, 0)

    for stage in (0, 1, 3):
        for s in (1, 2, 3):
            meta_copy(stage, s).wait_send()
    meta_copy(2, 1).wait_send()

    def drain(i, carry):
        for half in (0, 1):
            c = 2 * i + half
            for s in (1, 2, 3):
                first(c, half, s).wait_send()
            opposite(c).wait_send()
            for d in (0, 1):
                spread(c, d).wait_send()
                spread_on(c, d).wait_send()
                second(c, half, d).wait_send()
                onward(c, half, d).wait_send()
            for b in range(1, 6):
                near(c, b).wait_send()
            for j in range(1, 8):
                near_far(c, j).wait_send()
        return carry

    lax.fori_loop(0, pairs, drain, 0)


def return_kernel(
    pairs,
    h_in, hs_in, comb_in, comb_far_in, w_down, s_down,
    out,
    h, hs, comb, comb_far, in_sem,
    down_v, sd_v, snd, rcv, rcv_two, snd_far, rcv_far, part, relay, got1, half_sum, got2, part_far, relay_far, got_far, sum_far, got_home,
    load_sem, z_send, z_recv, y_send, y_recv, r0_send, r0_recv, r1_send, r1_recv, r2_send, r2_recv,
    f_send, f_recv, g_send, g_recv, a_send, a_recv,
):
    here = Place()
    x, y = here.x, here.y
    n = 2 * pairs

    def load(i, which):
        columns = pl.ds(pl.multiple_of(i * 2 * W, 2 * W), 2 * W)
        src, dst = (
            (w_down.at[0, :, columns], down_v.at[i]),
            (s_down.at[:, columns], sd_v.at[i]),
        )[which]
        return pltpu.make_async_copy(src, dst, load_sem.at[which, i])

    def start_loads(i, carry):
        for which in (0, 1):
            load(i, which).start()
        return carry

    brought = [
        pltpu.make_async_copy(src, dst, in_sem.at[k])
        for k, (src, dst) in enumerate(((h_in, h), (hs_in, hs), (comb_in, comb), (comb_far_in, comb_far)))
    ]
    brought[0].start()
    load(0, 0).start()
    load(0, 1).start()
    for copy in brought[1:]:
        copy.start()
    lax.fori_loop(1, pairs, start_loads, 0)
    here.greet()
    for copy in brought:
        copy.wait()

    def lead(half):
        return ("y", "x") if half == 0 else ("x", "y")

    def place(axis, step=0):
        return lax.rem((x if axis == "x" else y) + step, 4)

    def near(c, b):
        dz, dc = NEAR[b]
        return remote(
            snd.at[c, b - 1], rcv.at[c, b], z_send.at[c, b - 1], z_recv.at[c, b - 1], here.at(0, 0, 4 - dz, dc)
        )

    def near_far(c, j):
        dy, dc = FAR[j]
        return remote(
            snd_far.at[c, j], rcv_far.at[c, j], y_send.at[c, j], y_recv.at[c, j], here.at(0, 4 - dy, 0, dc)
        )

    def near_two(c, j):
        dy, dc = FAR[j]
        rows = pl.ds(pl.multiple_of(lax.rem(y + 4 - dy, 4) * 32, 32), 32)
        return remote(
            snd_far.at[c, j], rcv_two.at[c, dc, rows], y_send.at[c, j], y_recv.at[c, j], here.at(0, 0, 2, dc)
        )

    def far_rows(c, what):
        def straight():
            for j in range(8):
                getattr(near_two(c, j), what)()

        def around():
            for j in (4, 5, 2, 3, 6, 7, 1):
                getattr(near_far(c, j), what)()

        when(c >= n - STRAIGHT_BACK, straight)
        when(c < n - STRAIGHT_BACK, around)

    def through(c, half, d):
        axis = lead(half)[0]
        block = line(part, c, axis, place(axis, 2), pl.ds(2 * d, 2))
        return remote(block, relay.at[c, d], r0_send.at[c, d], r0_recv.at[c, d], here.along(axis, 3 - 2 * d))

    def first(c, half, d):
        axis = lead(half)[0]
        block = line(part, c, axis, place(axis, 3 - 2 * d))
        return remote(block, got1.at[c, d], r1_send.at[c, d], r1_recv.at[c, d], here.along(axis, 3 - 2 * d))

    def second(c, half, s):
        axis = lead(half)[1]
        block = half_sum.at[c, place(axis, s)]
        return remote(block, got2.at[c, s - 1], r2_send.at[c, s - 1], r2_recv.at[c, s - 1], here.along(axis, s))

    def through_far(c, d):
        block = part_far.at[c, place("x", 2), pl.ds(32 * d, 32)]
        return remote(block, relay_far.at[c, d], g_send.at[c, d], g_recv.at[c, d], here.along("x", 3 - 2 * d))

    def gather_far(c, d):
        block = part_far.at[c, place("x", 3 - 2 * d)]
        return remote(block, got_far.at[c, d], f_send.at[c, d], f_recv.at[c, d], here.along("x", 3 - 2 * d))

    def home(c):
        return remote(sum_far.at[c], got_home.at[c], a_send.at[c], a_recv.at[c], here.at(0, 0, 2, 0))

    def down(c, half):
        i = lax.div(c, 2)
        if half == 0:
            load(i, 0).wait()
        for m in range(4):
            piece = dot(h[m * 256 : m * 256 + 256], down_v[i, :, half * W : half * W + W]).astype(BF16)
            if m == 3:
                piece = piece.reshape(8, 32, W)
                rcv_far[c, 0] = piece[0]
                snd_far[c] = piece
            elif m == 0:
                rcv[c, 0] = piece[:128]
                snd[c, 0] = piece[128:]
            else:
                snd[c, 2 * m - 1] = piece[:128]
                snd[c, 2 * m] = piece[128:]
        for b in range(1, 6):
            near(c, b).start()
        far_rows(c, "start")

    def combine(c, half):
        i = lax.div(c, 2)
        if half == 0:
            load(i, 1).wait()
        far_rows(c, "wait_recv")

        def far_part():
            total = dot(comb_far[...], rcv_far[c].reshape(256, W))
            part_far[c] = total.astype(BF16).reshape(4, 64, W)
            for d in (0, 1):
                through_far(c, d).start()

        def near_part(count):
            for q in range(4):
                span = slice(q * 32, q * 32 + 32)
                rows = [sd_v[i, :, half * W : half * W + W], rcv[c, :, span].reshape(192, W)]
                if count == 8:
                    rows.append(rcv_two[c, :, span].reshape(64, W))
                left = jnp.concatenate([hs[q * 256 : q * 256 + 256], comb[q, :, : count * 32]], axis=1)
                part[c, q] = dot(left, jnp.concatenate(rows, axis=0)).astype(BF16).reshape(4, 64, W)

        when(c < n - STRAIGHT_BACK, far_part)
        for b in range(1, 6):
            near(c, b).wait_recv()
        when(c < n - STRAIGHT_BACK, lambda: near_part(6))
        when(c >= n - STRAIGHT_BACK, lambda: near_part(8))
        for d in (0, 1):
            through(c, half, d).start()

    def pass_on(c, half):
        axis = lead(half)[0]
        for d in (0, 1):
            through(c, half, d).wait_recv()
            target = place(axis, 3 - 2 * d)
            for b in (2 * d, 2 * d + 1):
                where = (c, target, b) if axis == "y" else (c, b, target)
                part[where] = (part[where].astype(F32) + relay[c, d, b - 2 * d].astype(F32)).astype(BF16)
        for d in (0, 1):
            first(c, half, d).start()

        def go():
            for d in (0, 1):
                through_far(c, d).wait_recv()
                where = (c, place("x", 3 - 2 * d), slice(32 * d, 32 * d + 32))
                part_far[where] = (part_far[where].astype(F32) + relay_far[c, d].astype(F32)).astype(BF16)
            for d in (0, 1):
                gather_far(c, d).start()

        when(c < n - STRAIGHT_BACK, go)

    def reduce(c, half):
        for d in (0, 1):
            first(c, half, d).wait_recv()
        for b in range(4):
            mine = part[c, y, b] if half == 0 else part[c, b, x]
            total = mine.astype(F32) + got1[c, 0, b].astype(F32) + got1[c, 1, b].astype(F32)
            half_sum[c, b] = total.astype(BF16)
        for s in (2, 1, 3):
            second(c, half, s).start()

        def send_home():
            total = part_far[c, x].astype(F32)
            for d in (0, 1):
                gather_far(c, d).wait_recv()
                total += got_far[c, d].astype(F32)
            sum_far[c] = total.astype(BF16)
            home(c).start()

        when(c < n - STRAIGHT_BACK, send_home)

    def final(c, half):
        total = half_sum[c, place(lead(half)[1])].astype(F32)
        for s in (1, 2, 3):
            second(c, half, s).wait_recv()
            total += got2[c, s - 1].astype(F32)

        def with_far():
            home(c).wait_recv()
            out[:, chunk(c)] = (total + got_home[c].astype(F32)).astype(BF16)

        def without():
            out[:, chunk(c)] = total.astype(BF16)

        when(c < n - STRAIGHT_BACK, with_far)
        when(c >= n - STRAIGHT_BACK, without)

    def step(i, carry):
        for half in (0, 1):
            c = 2 * i + half
            for stage, lag in ((down, 0), (pass_on, PASS), (reduce, REDUCE), (final, FINAL), (combine, COMBINE)):

                @pl.when((c >= lag) & (c < n + lag))
                def _():
                    stage(c - lag, (half + lag) % 2)

        return carry

    lax.fori_loop(0, pairs + (FINAL + 1) // 2, step, 0)

    def drain(i, carry):
        for half in (0, 1):
            c = 2 * i + half
            for d in (0, 1):
                through(c, half, d).wait_send()
                first(c, half, d).wait_send()
            for s in (1, 2, 3):
                second(c, half, s).wait_send()

            def sent():
                for d in (0, 1):
                    through_far(c, d).wait_send()
                    gather_far(c, d).wait_send()
                home(c).wait_send()

            when(c < n - STRAIGHT_BACK, sent)
            for b in range(1, 6):
                near(c, b).wait_send()
            far_rows(c, "wait_send")
        return carry

    lax.fori_loop(0, pairs, drain, 0)


def shards(
    tokens, route_ids, route_weight, w_gate, w_up, w_down, shared_gate, shared_up, shared_down
):
    width = tokens.shape[1]
    pairs = width // (2 * W)
    n = 2 * pairs
    vmem = pl.BlockSpec(memory_space=pltpu.VMEM)
    hbm = pl.BlockSpec(memory_space=pl.ANY)

    def both(*shape):
        return [pltpu.SemaphoreType.DMA(shape)] * 2

    def held(*shape, dtype=BF16):
        return pltpu.VMEM(shape, dtype)

    hidden, shared_hidden, comb, comb_far = pl.pallas_call(
        functools.partial(dispatch_kernel, pairs),
        out_shape=(
            jax.ShapeDtypeStruct((1024, 1024), BF16),
            jax.ShapeDtypeStruct((1024, 128), BF16),
            jax.ShapeDtypeStruct((4, 256, 256), BF16),
            jax.ShapeDtypeStruct((256, 256), BF16),
        ),
        in_specs=[vmem] * 3 + [hbm] * 4,
        out_specs=(vmem,) * 4,
        scratch_shapes=[
            held(n, 4, 4, 64, W),
            held(n, 4, 64, W),
            held(n, 5, 128, W),
            held(n, 6, 128, W),
            held(n, 7, 32, W),
            held(n, 8, 32, W),
            held(1024, 1024, dtype=F32),
            held(1024, 1024, dtype=F32),
            held(pairs, 2 * W, 1024),
            held(pairs, 2 * W, 1024),
            held(pairs, 2 * W, 256),
            held(64, 128, dtype=F32),
            held(4, 4, 64, 128, dtype=F32),
            held(4, 64, 128, dtype=F32),
            held(4, 256, 256),
            held(256, 256),
            held(1024, 256, dtype=F32),
            pltpu.SemaphoreType.DMA((4, pairs)),
            *both(4, 3), *both(n, 3), *both(n, 2), *both(n, 2),
            *both(n), *both(n, 2), *both(n, 2), *both(n, 5), *both(n, 7),
        ],
        compiler_params=pltpu.CompilerParams(
            collective_id=0, has_side_effects=True, vmem_limit_bytes=60 * 2**20
        ),
        name="dispatch",
    )(tokens, route_ids.T, route_weight.T, w_gate, w_up, shared_gate, shared_up)
    return pl.pallas_call(
        functools.partial(return_kernel, pairs),
        out_shape=jax.ShapeDtypeStruct((64, width), BF16),
        in_specs=[hbm] * 6,
        out_specs=vmem,
        scratch_shapes=[
            held(1024, 1024),
            held(1024, 128),
            held(4, 256, 256),
            held(256, 256),
            pltpu.SemaphoreType.DMA((4,)),
            held(pairs, 1024, 2 * W),
            held(pairs, 128, 2 * W),
            held(n, 5, 128, W),
            held(n, 6, 128, W),
            held(n, 2, 128, W),
            held(n, 8, 32, W),
            held(n, 8, 32, W),
            held(n, 4, 4, 64, W),
            held(n, 2, 2, 64, W),
            held(n, 2, 4, 64, W),
            held(n, 4, 64, W),
            held(n, 3, 64, W),
            held(n, 4, 64, W),
            held(n, 2, 32, W),
            held(n, 2, 64, W),
            held(n, 64, W),
            held(n, 64, W),
            pltpu.SemaphoreType.DMA((2, pairs)),
            *both(n, 5), *both(n, 8), *both(n, 2), *both(n, 2), *both(n, 3),
            *both(n, 2), *both(n, 2), *both(n),
        ],
        compiler_params=pltpu.CompilerParams(
            collective_id=1, has_side_effects=True, vmem_limit_bytes=60 * 2**20
        ),
        name="bring_back",
    )(hidden, shared_hidden, comb, comb_far, w_down, shared_down)


def solution(mesh):
    in_specs = (
        P(("ex", "ey"), None),
        P(("ex", "ey"), None),
        P(("ex", "ey"), None),
        P(("ex", "ey"), None, None),
        P(("ex", "ey"), None, None),
        P(("ex", "ey"), None, None),
        P(None, "ex"),
        P(None, "ex"),
        P("ex", None),
    )
    out_specs = P(("ex", "ey"), None)
    return jax.shard_map(shards, mesh=mesh, in_specs=in_specs, out_specs=out_specs, check_vma=False)
```
